32 devices in a mesh: cube: 4 (over z), row: 2 (over y), col: 4 (over x, core).
Axes of the slice: x: 2, y: 2, z: 4, core: 2. Of those that a mesh axis runs over, the one named last changes fastest.
Arguments:
- diag_block: float32 [4, 512, 512], P('cube', ('row', 'col')), may hold values from -1 to 4, as said below
- panel: float32 [4, 16384, 512], P('cube', 'row', 'col'), may hold values from -2 to 2
- pattern: int32 [4, 128, 4], P('cube', 'row', 'col'), may hold values 0 or 1
- contribution: float32 [4, 16384, 512], P('cube', 'row', 'col'), may hold values from -6 to 6
- route: int32 [4, 128, 1], P('cube', 'row'), may hold values from 0 to 3; in each aligned block of 64 rows (0 to 63, 64 to 127, ..., all dimensions but the last counted through in order) at most 32 rows name the same one
- slot: int32 [4, 128], P('cube', 'row'), may hold values from 0 to 31
Outputs:
- diag_factor: float32 [4, 512, 512], P('cube', ('row', 'col'))
- panel_factor: float32 [4, 16384, 512], P('cube', 'row', 'col')
- assembled: float32 [4, 8192, 512], P('cube', 'row', 'col')
The draws below stay inside these ranges and needn't reach their ends.
Inputs may be any that keep to these rules, and one draw needn't show every extreme that they name: `diag_block`: each 512 x 512 block is symmetric with positive diagonal larger than the sum of magnitudes of the rest of its row. `route`: within the 64 rows of one device, no value names more than 32 blocks.
All inputs are finite; a program needn't handle non-finite values. No bound on the sum of `pattern` on one device may be relied on, other than what follows from the above.
Results may differ from the reference program's by a relative error of at most 0.0001.
Values sent between devices are 32-bit elements; how exact they have to be, the bound alone decides.
A program may use at most 128 MiB of HBM per device.

```python
import math
import jax
import jax.numpy as jnp
import numpy as np
from jax import lax

PB = 512
M = 16384
BS = 128
CW = 512
FRONTS = 4
MB = 128
BLK_DEV = 64
CAP = 32
PBLK = 32
N_CUBE = 4
N_ROW = 2


def draw_diag_block(key, part):
    first = jax.random.fold_in(jax.random.fold_in(key, 11), 0)
    second = jax.random.fold_in(jax.random.fold_in(key, 11), 1)
    fourth = jax.random.fold_in(jax.random.fold_in(key, 11), 3)
    ident = jnp.eye(PB, dtype=jnp.float32)[None]
    index_rows = jnp.arange(PB, dtype=jnp.int32)[:, None]
    index_cols = jnp.arange(PB, dtype=jnp.int32)[None, :]
    distance = jnp.abs(index_rows - index_cols)
    heights = jax.random.uniform(second, (N_CUBE, PB), jnp.float32, 2.5, 3.5)
    coupling = jax.random.uniform(first, (N_CUBE, PB, PB), jnp.float32, 0.5, 1.0)
    coupling = 0.5 * (coupling + jnp.swapaxes(coupling, 1, 2))
    banded = ((distance >= 1) & (distance <= 3)).astype(jnp.float32)[None]
    scatter = jax.random.uniform(fourth, (N_CUBE, PB, PB), jnp.float32, -1.0, 1.0)
    scatter = 0.5 * (scatter + jnp.swapaxes(scatter, 1, 2))
    offdiag = coupling * banded * 0.36 + scatter * (0.3 / PB)
    return offdiag * (1.0 - ident) + ident * heights[:, :, None]


def set_ends(result, own_key, low, largest):
    spot = [jax.random.randint(jax.random.fold_in(own_key, axis), (), 0, length) for axis, length in enumerate(result.shape)]
    main_axis = result.shape.index(max(result.shape))
    neighbour = spot[:main_axis] + [(spot[main_axis] + 1) % result.shape[main_axis]] + spot[main_axis + 1:]
    return result.at[tuple(spot)].set(low).at[tuple(neighbour)].set(largest)


def level_of(key, extent, pieces, smallest, high):
    factor_of = 1.0
    for dim, blocks in pieces:
        steps = jax.random.uniform(jax.random.fold_in(jax.random.fold_in(key, 6), dim), (blocks,), jnp.float32, smallest / len(pieces), high / len(pieces))
        factor_of = factor_of * jnp.repeat(jnp.exp(steps), extent[dim] // blocks).reshape((-1,) + (1,) * (len(extent) - 1 - dim))
    return factor_of


def deal_out(own_key, own, number, rows, number_of, top, limit, slope):
    order = jax.random.permutation(own_key, number_of)
    packed, common = shares(number_of, rows * top, limit, slope, True), shares(number_of, rows * top, limit, slope, False)
    places = jnp.arange(number_of)

    def named(tallies, rotation):
        used = int((tallies > 0).sum())
        fixed = max(1, used // 4)
        shifted = fixed + (places - fixed + rotation * (used - fixed)) % max(1, number_of - fixed)
        return jnp.zeros((number_of,), jnp.int32).at[order[jnp.where(places < fixed, places, shifted)]].set(jnp.asarray(tallies, jnp.int32))

    tallies = jnp.where(number % 4 == 0, named(packed, number // 4), named(common, number - number // 4 - 1))
    mixed = jax.random.permutation(jax.random.fold_in(own, 3), number_of)
    donor, sink = mixed[0:number_of // 2 * 2:2], mixed[1:number_of // 2 * 2:2]
    margin = jnp.minimum(tallies[donor] - 1, limit - tallies[sink]) // 2
    margin = jnp.where((donor == order[0]) | (sink == order[0]) | (tallies[sink] == 0), 0, jnp.maximum(margin, 0))
    shifted = jax.random.randint(jax.random.fold_in(own, 4), (number_of // 2,), 0, 1 << 20) % (margin + 1)
    tallies = tallies.at[donor].add(-shifted).at[sink].add(shifted)
    labels = jnp.searchsorted(jnp.cumsum(tallies), jnp.arange(rows * top), side="right").astype(jnp.int32)
    listing = labels.reshape(top, rows).T
    listing = listing[jax.random.permutation(jax.random.fold_in(own, 1), rows)]
    rotation = jax.random.randint(jax.random.fold_in(own, 2), (rows, 1), 0, top)
    return jnp.take_along_axis(listing, (jnp.arange(top)[None, :] + rotation) % top, axis=1)


def shares(amount, total, bound, lean, full):
    portions = [(1 << 20) // math.isqrt(grade ** lean) + 1 for grade in range(1, amount + 1)]
    largest = bound if full else min(bound, max(-(-total // amount), total * portions[0] // sum(portions)))
    least = 1 if total - largest >= amount - 1 else 0
    given, rest = [largest] + [least] * (amount - 1), total - largest - least * (amount - 1)
    while rest > 0:
        candidates = [i for i in range(1, amount) if given[i] < largest] or [i for i in range(1, amount) if given[i] < bound]
        whole, budget = sum([portions[i] for i in candidates]), rest
        for i in candidates:
            extra = min(bound - given[i], max(1, budget * portions[i] // whole), rest)
            given[i] = given[i] + extra
            rest = rest - extra
    return np.array(given)


def noise(stream_key, shape, spread, bound, pieces=(), kind=jnp.bfloat16):
    level = level_of(stream_key, shape, pieces, -0.22, 0.18) if pieces else 1.0
    values = jax.random.normal(stream_key, shape, jnp.float32) * spread * level
    return jnp.minimum(jnp.maximum(values, -bound), bound).astype(kind)


def setup_inputs(seed: int = 0) -> dict:
    splits = jax.random.split(jax.random.key(seed), 7)
    diag_block = draw_diag_block(jax.random.fold_in(splits[6], 71), 0)
    panel = noise(splits[1], (FRONTS, M, PB), (max(1, PB // 64)) ** -0.5, 2.0, ((0, 4), (1, 2), (2, 4)), jnp.float32)
    pattern = set_ends((jax.random.randint(splits[2], (FRONTS, MB, PB // BS), 0, 4) < 3).astype(jnp.int32), jax.random.fold_in(splits[2], 1), 0, 1)
    contribution = noise(splits[3], (FRONTS, M, CW), 1.0, 6.0, ((0, 4), (1, 2), (2, 4)), jnp.float32)
    route_keys = jax.random.split(jax.random.fold_in(splits[4], 1), FRONTS * MB // BLK_DEV)
    route_turns = jax.random.permutation(jax.random.fold_in(splits[4], 3), FRONTS * MB // BLK_DEV)
    route = jax.vmap(lambda own, number: deal_out(jax.random.fold_in(splits[4], 2), own, number, BLK_DEV, 2 * N_ROW, 1, CAP, 0))(route_keys, route_turns).reshape((FRONTS, MB, 1))
    slot = set_ends(jax.random.randint(splits[5], (FRONTS, MB), 0, PBLK), jax.random.fold_in(splits[5], 1), 0, PBLK - 1).astype(jnp.int32)
    return {"diag_block": diag_block, "panel": panel, "pattern": pattern, "contribution": contribution, "route": route, "slot": slot}


def reference(diag_block, panel, pattern, contribution, route, slot):
    highest = lax.Precision.HIGHEST
    factors = []
    panels = []
    updates = []
    for front in range(N_CUBE):
        lower = jnp.linalg.cholesky(diag_block[front])
        inverse = jax.scipy.linalg.solve_triangular(lower, jnp.eye(PB, dtype=jnp.float32), lower=True)
        tile_mask = jnp.repeat(jnp.repeat(pattern[front], BS, axis=0), BS, axis=1).astype(jnp.float32)
        masked = panel[front] * tile_mask
        factor_rows = jnp.dot(masked, inverse.T, precision=highest)
        update = contribution[front] - jnp.dot(factor_rows, factor_rows[:CW].T, precision=highest)
        factors.append(lower)
        panels.append(factor_rows)
        updates.append(update)
    halves = []
    for parent_index in range(N_CUBE // 2):
        total = jnp.zeros((MB, BS * CW), jnp.float32)
        for child in (2 * parent_index, 2 * parent_index + 1):
            blocks = updates[child].reshape(MB, BS * CW)
            target = (route[child, :, 0] * PBLK + slot[child]).astype(jnp.int32)
            total = total.at[target].add(blocks)
        total = total.reshape(2, M // 2, CW)
        halves.append(total[0])
        halves.append(total[1])
    return (jnp.stack(factors), jnp.stack(panels), jnp.stack(halves))
```

```python
import functools

import jax
import jax.numpy as jnp
from jax import lax
from jax.experimental import pallas as pl
from jax.experimental.pallas import tpu as pltpu
from jax.sharding import PartitionSpec as P

BS = 128
HIGHEST = lax.Precision.HIGHEST
NT = (((1,), (1,)), ((), ()))
ANY = pl.BlockSpec(memory_space=pl.ANY)
VMEM = pl.BlockSpec(memory_space=pltpu.VMEM)
SMEM = pl.BlockSpec(memory_space=pltpu.SMEM)
MESH = pl.DeviceIdType.MESH


def remote(src, dst, send, recv, device):
    return pltpu.make_async_remote_copy(
        src_ref=src, dst_ref=dst, send_sem=send, recv_sem=recv,
        device_id=device, device_id_type=MESH,
    )


def column(s, j):
    return jnp.take_along_axis(s, jnp.full(s.shape, j, jnp.int32), axis=1)


def factor_block(s_ref, x_ref):
    n = BS
    sub = lax.broadcasted_iota(jnp.int32, (n, n), 0)
    lane = lax.broadcasted_iota(jnp.int32, (n, n), 1)
    s = s_ref[...]
    x = (sub == lane).astype(jnp.float32)
    for k in range(n // 8):
        row = lax.broadcasted_iota(jnp.int32, s.shape, 0)
        for t in range(0, 8, 2):
            c0, c1 = column(s, 8 * k + t), column(s, 8 * k + t + 1)
            s0, s1, x0, x1 = s[t:t + 1], s[t + 1:t + 2], x[t:t + 1], x[t + 1:t + 2]
            a, b, d = c0[t:t + 1], c1[t:t + 1], c1[t + 1:t + 2]
            inv = 1.0 / (a * d - b * b)
            below = row > t + 1
            m0 = jnp.where(below, (c0 * d - c1 * b) * inv, jnp.where(row == t + 1, b / a, 0.0))
            m1 = jnp.where(below, (c1 * a - c0 * b) * inv, 0.0)
            s = s - (m0 * s0 + m1 * s1)
            x = x - (m0 * x0 + m1 * x1)
        s_ref[8 * k:8 * k + 8, :] = s[:8]
        x_ref[8 * k:8 * k + 8, :] = x[:8]
        s, x = s[8:], x[8:]


def cholesky_inverse(a_ref, inv_ref, s_ref, x_ref, between):
    width = a_ref.shape[0]
    sub = lax.broadcasted_iota(jnp.int32, (BS, BS), 0)
    lane = lax.broadcasted_iota(jnp.int32, (BS, BS), 1)
    inv_ref[...] = jnp.zeros_like(inv_ref)
    for p in range(width // BS):
        o, e = p * BS, (p + 1) * BS
        s_ref[...] = a_ref[o:e, o:e]
        factor_block(s_ref, x_ref)
        s = s_ref[...]
        d = jnp.sum(jnp.where(lane == sub, s, 0.0), axis=1, keepdims=True)
        rs = 1.0 / jnp.sqrt(d)
        low = jnp.transpose(jnp.where(lane >= sub, s, 0.0) * rs)
        x = x_ref[...] * rs
        a_ref[o:e, o:e] = low
        inv_ref[o:e, o:e] = x
        if e < width:
            below = lax.dot_general(a_ref[e:, o:e], x, NT, precision=HIGHEST)
            a_ref[e:, o:e] = below
            a_ref[e:, e:] = a_ref[e:, e:] - lax.dot_general(below, below, NT, precision=HIGHEST)
            a_ref[o:e, e:] = jnp.zeros((BS, width - e), jnp.float32)
        if p > 0:
            part = jnp.dot(a_ref[o:e, :o], inv_ref[:o, :o], precision=HIGHEST)
            inv_ref[o:e, :o] = -jnp.dot(x, part, precision=HIGHEST)
        between(p)


def gather_kernel(rows, prev_ref, prev_on, last_ref, last_on, diag_ref, mask_ref, panel_ref, contribution_ref,
                  f_ref, out_ref, l_ref,
                  own, g0, g1, g2, contrib, a_ref, inv_ref, s_ref, x_ref, h_ref, hc_ref, w_ref,
                  vh_ref, vl_ref, masks, head_masks, upd, t_ref, ra, rb, ra2, rb2,
                  dsend, drecv, xsend, xrecv, fsend, frecv, psend, precv, hsend, hrecv,
                  msend, mrecv, isem, asend, arecv, bsend, brecv, lsend, lrecv):
    z = lax.axis_index("cube")
    m = z % 2
    r, c = lax.axis_index("row"), lax.axis_index("col")
    y = 1 - r
    c1 = c + 1 - 2 * (c % 2)
    c2 = (c + 2) % 4
    c3 = (c1 + 2) % 4
    order = (c, c1, c2, c3)
    pieces = (own, g0, g1, g2)
    ndiag = diag_ref.shape[0]
    blocks = panel_ref.shape[0]
    slices = BS // rows
    slots = out_ref.shape[0]
    half = slots // 2
    heads = a_ref.shape[0] // BS
    to_x, to_core, to_row = {"col": c2}, {"col": c1}, {"row": y}
    to_cube = {"cube": z + 1 - 2 * m}

    load_own = pltpu.make_async_copy(panel_ref, own, isem.at[0])
    load_contrib = pltpu.make_async_copy(contribution_ref, contrib, isem.at[1])
    barrier = pltpu.get_barrier_semaphore()
    for device in (to_x, to_core, to_row, to_cube):
        pl.semaphore_signal(barrier, inc=1, device_id=device, device_id_type=MESH)
    pl.semaphore_wait(barrier, 4)

    def spot(rr, cc):
        return a_ref.at[pl.ds(pl.multiple_of((rr * 4 + cc) * ndiag, ndiag), ndiag)]

    def diag_copy(k, src, rr, cc, device):
        return remote(src, spot(rr, cc), dsend.at[k], drecv.at[k], device)

    def sliced(i):
        return (pl.ds(heads, blocks - heads), pl.ds(pl.multiple_of(i * rows, rows), rows))

    top = (pl.ds(0, heads),)

    def across(i, part):
        return remote(panel_ref.at[part], g1.at[part], xsend.at[i], xrecv.at[i], to_x)

    def onward(i, part):
        return remote(g1.at[part], g2.at[part], fsend.at[i], frecv.at[i], to_core)

    def beside(i, part):
        return remote(panel_ref.at[part], g0.at[part], psend.at[i], precv.at[i], to_core)

    mask_x = remote(mask_ref, masks.at[2], msend.at[0], mrecv.at[0], to_x)
    mask_core = remote(mask_ref, masks.at[1], msend.at[1], mrecv.at[1], to_core)
    mask_on = remote(masks.at[2], masks.at[3], msend.at[2], mrecv.at[2], to_core)

    first = diag_copy(0, diag_ref, r, c, to_x)
    first.start()
    mask_x.start()
    across(slices, top).start()
    for i in range(slices):
        across(i, sliced(i)).start()
    second = [diag_copy(1, diag_ref, r, c, to_row)]
    second[0].start()
    mask_core.start()
    load_own.start()
    load_contrib.start()
    a_ref[pl.ds(pl.multiple_of((r * 4 + c) * ndiag, ndiag), ndiag), :] = diag_ref[...]
    masks[0] = mask_ref[...]
    first.wait_recv()
    second.append(diag_copy(2, spot(r, c2), r, c2, to_row))
    second[1].start()
    third = [
        diag_copy(3, diag_ref, r, c, to_core),
        diag_copy(4, spot(r, c2), r, c2, to_core),
    ]
    for copy in third:
        copy.start()
    mask_x.wait_recv()
    mask_on.start()
    for copy in second:
        copy.wait_recv()
    third.append(diag_copy(5, spot(y, c), y, c, to_core))
    third.append(diag_copy(6, spot(y, c2), y, c2, to_core))
    for copy in third[2:]:
        copy.start()
    for copy in third:
        copy.wait_recv()
    for copy in [first] + second + third:
        copy.wait_send()
    beside(slices, top).start()
    across(slices, top).wait_recv()
    onward(slices, top).start()
    for i in range(slices):
        beside(i, sliced(i)).start()
    head = [remote(piece.at[c], h_ref.at[j], hsend.at[j], hrecv.at[j], to_row) for j, piece in enumerate(pieces)]
    head_mask = remote(masks, head_masks, hsend.at[4], hrecv.at[4], to_row)

    def between(p):
        if p != 0:
            return
        load_own.wait()
        load_contrib.wait()
        beside(slices, top).wait_recv()
        onward(slices, top).wait_recv()
        mask_core.wait_recv()
        mask_on.wait_recv()

        @pl.when(r == 0)
        def _():
            for copy in head:
                copy.start()
            head_mask.start()
            for j, k in enumerate(order):
                hc_ref[:, pl.ds(pl.multiple_of(k * BS, BS), BS)] = pieces[j][c] * masks[j, pl.ds(c, 1), :]

    cholesky_inverse(a_ref, inv_ref, s_ref, x_ref, between)
    l_ref[...] = a_ref[pl.ds(pl.multiple_of((r * 4 + c) * ndiag, ndiag), ndiag), :]

    @pl.when(r == 0)
    def _():
        for copy in head:
            copy.wait_send()
        head_mask.wait_send()

    @pl.when(r == 1)
    def _():
        for copy in head:
            copy.wait_recv()
        head_mask.wait_recv()
        for j, k in enumerate(order):
            hc_ref[:, pl.ds(pl.multiple_of(k * BS, BS), BS)] = h_ref[j] * head_masks[j, pl.ds(c, 1), :]

    factor_head = lax.dot_general(hc_ref[...], inv_ref[...], NT, precision=HIGHEST)
    w_ref[pl.ds(BS, BS), :] = jnp.dot(factor_head, inv_ref[...], precision=HIGHEST)
    w_ref[pl.ds(0, BS), :] = inv_ref[pl.ds(pl.multiple_of(c * BS, BS), BS), :]
    for j, k in enumerate(order):
        high, low = split(jnp.transpose(w_ref[:, pl.ds(pl.multiple_of(k * BS, BS), BS)]))
        vh_ref[j * BS:(j + 1) * BS, :] = high
        vl_ref[j * BS:(j + 1) * BS, :] = low

    group = min(blocks, 512 // rows)

    def compute(i):
        part = pl.ds(pl.multiple_of(i * rows, rows), rows)

        def tile(q, carry):
            lines = []
            for b in range(group):
                at = q * group + b
                lines.append(jnp.concatenate(
                    [piece[at, part] * masks[j, pl.ds(at, 1), :] for j, piece in enumerate(pieces)], axis=1))
            high, low = split(jnp.concatenate(lines, axis=0))
            dot = functools.partial(jnp.dot, preferred_element_type=jnp.float32)
            out = dot(high, vh_ref[...]) + (dot(high, vl_ref[...]) + dot(low, vh_ref[...]))
            for b in range(group):
                at = q * group + b
                f_ref[at, part] = out[b * rows:(b + 1) * rows, :BS]
                update = contrib[at, part] - out[b * rows:(b + 1) * rows, BS:]
                upd[at] = update + prev_on[at] * upd[prev_ref[at]]
            return carry

        lax.fori_loop(0, blocks // group, tile, 0)

        def fill(q, carry):
            for b in range(8):
                k = q * 8 + b
                t_ref[k, part] = upd[last_ref[k]] * last_on[k]
            return carry

        lax.fori_loop(0, 4 * slots // 8, fill, 0)

    def quarter(g, low):
        return pl.ds(g * slots + (0 if low else half), half)

    def hops(i):
        part = pl.ds(pl.multiple_of(i * rows, rows), rows)
        goal = ((1 - m) * 2 + y, m * 2 + y, (1 - m) * 2 + r)
        over_a = [remote(t_ref.at[quarter(goal[k], True), part], ra.at[k, :, part],
                         asend.at[k, i], arecv.at[k, i], to_row) for k in range(2)]
        over_b = [remote(t_ref.at[quarter(goal[2 * k], False), part], rb.at[k, :, part],
                         bsend.at[k, i], brecv.at[k, i], to_cube) for k in range(2)]
        last = [remote(ra.at[0, :, part], ra2.at[:, part], lsend.at[0, i], lrecv.at[0, i], to_cube),
                remote(rb.at[0, :, part], rb2.at[:, part], lsend.at[1, i], lrecv.at[1, i], to_row)]
        return part, over_a, over_b, last

    def turn(i):
        part, over_a, over_b, last = hops(i)
        over_a[0].wait_recv()
        ra[0, :, part] = ra[0, :, part] + t_ref[quarter((1 - m) * 2 + r, True), part]
        last[0].start()
        over_b[0].wait_recv()
        rb[0, :, part] = rb[0, :, part] + t_ref[quarter(m * 2 + y, False), part]
        last[1].start()

    def finish(i):
        part, over_a, over_b, last = hops(i)
        over_a[1].wait_recv()
        last[0].wait_recv()
        out_ref[pl.ds(0, half), part] = t_ref[quarter(m * 2 + r, True), part] + ra[1, :, part] + ra2[:, part]
        over_b[1].wait_recv()
        last[1].wait_recv()
        out_ref[pl.ds(half, half), part] = t_ref[quarter(m * 2 + r, False), part] + rb[1, :, part] + rb2[:, part]

    upd[...] = jnp.zeros_like(upd)

    def step(i, carry):
        @pl.when(i < slices)
        def _():
            across(i, sliced(i)).wait_recv()
            onward(i, sliced(i)).start()
            beside(i, sliced(i)).wait_recv()
            onward(i, sliced(i)).wait_recv()
            compute(i)
            _, over_a, over_b, _ = hops(i)
            for k in range(2):
                over_a[k].start()
                over_b[k].start()

        @pl.when((i > 0) & (i <= slices))
        def _():
            turn(i - 1)

        @pl.when(i > 1)
        def _():
            finish(i - 2)
        return carry

    lax.fori_loop(0, slices + 2, step, 0)

    def drain(i, carry):
        _, over_a, over_b, last = hops(i)
        for copy in over_a + over_b + last + [across(i, sliced(i)), onward(i, sliced(i)), beside(i, sliced(i))]:
            copy.wait_send()
        return carry

    lax.fori_loop(0, slices, drain, 0)
    for copy in (across(slices, top), onward(slices, top), beside(slices, top), mask_x, mask_core, mask_on):
        copy.wait_send()


def factor_and_route(chains, diag, mask, panel, contribution, pblk):
    rows = 16
    slices = BS // rows
    tall, share = panel.shape
    blk = tall // BS
    half = pblk // 2
    ndiag, width = diag.shape
    whole = pltpu.VMEM((blk, BS, share), jnp.float32)
    square = pltpu.VMEM((width, width), jnp.float32)
    block = pltpu.VMEM((BS, BS), jnp.float32)
    sems = pltpu.SemaphoreType.DMA
    return pl.pallas_call(
        functools.partial(gather_kernel, rows),
        out_shape=(
            jax.ShapeDtypeStruct((blk, BS, share), jnp.float32),
            jax.ShapeDtypeStruct((pblk, BS, share), jnp.float32),
            jax.ShapeDtypeStruct((ndiag, width), jnp.float32),
        ),
        in_specs=[SMEM, SMEM, SMEM, SMEM, VMEM, VMEM, ANY, ANY],
        out_specs=(VMEM, VMEM, VMEM),
        scratch_shapes=[
            whole, whole, whole, whole, whole,
            square, square, block, block,
            pltpu.VMEM((4, BS, BS), jnp.float32),
            pltpu.VMEM((BS, width), jnp.float32),
            pltpu.VMEM((2 * BS, width), jnp.float32),
            pltpu.VMEM((width, 2 * BS), jnp.bfloat16),
            pltpu.VMEM((width, 2 * BS), jnp.bfloat16),
            pltpu.VMEM((4,) + mask.shape, jnp.float32),
            pltpu.VMEM((4,) + mask.shape, jnp.float32),
            pltpu.VMEM((blk, rows, share), jnp.float32),
            pltpu.VMEM((4 * pblk, BS, share), jnp.float32),
            pltpu.VMEM((2, half, BS, share), jnp.float32),
            pltpu.VMEM((2, half, BS, share), jnp.float32),
            pltpu.VMEM((half, BS, share), jnp.float32),
            pltpu.VMEM((half, BS, share), jnp.float32),
            sems((7,)), sems((7,)),
            sems((slices + 1,)), sems((slices + 1,)), sems((slices + 1,)), sems((slices + 1,)),
            sems((slices + 1,)), sems((slices + 1,)), sems((5,)), sems((5,)), sems((3,)), sems((3,)),
            sems((2,)),
            sems((2, slices)), sems((2, slices)), sems((2, slices)), sems((2, slices)),
            sems((2, slices)), sems((2, slices)),
        ],
        compiler_params=pltpu.CompilerParams(
            collective_id=0, has_side_effects=True, vmem_limit_bytes=54 * 2**20),
        name="gather_factor",
    )(*chains, diag, mask, panel.reshape(blk, BS, share), contribution.reshape(blk, BS, share))


def split(value):
    high = value.astype(jnp.bfloat16)
    return high, (value - high.astype(jnp.float32)).astype(jnp.bfloat16)


def on_small(diag_block, panel, pattern, contribution, route, slot):
    rows, share = panel.shape[1:]
    blk = rows // BS
    pblk = blk // 2
    nrow = lax.axis_size("row")
    mask = jnp.broadcast_to(pattern[0].astype(jnp.float32), (blk, share))
    goal = (route[0, :, 0] * pblk + slot[0]).astype(jnp.int32)
    ids = jnp.arange(blk, dtype=jnp.int32)
    earlier = (goal[None, :] == goal[:, None]) & (ids[None, :] < ids[:, None])
    prev = jnp.max(jnp.where(earlier, ids[None, :] + 1, 0), axis=1)
    names = jnp.arange(2 * nrow * pblk, dtype=jnp.int32)
    last = jnp.max(jnp.where(goal[None, :] == names[:, None], ids[None, :] + 1, 0), axis=1)
    chains = (
        jnp.maximum(prev - 1, 0), jnp.minimum(prev, 1).astype(jnp.float32),
        jnp.maximum(last - 1, 0), jnp.minimum(last, 1).astype(jnp.float32),
    )
    factor, assembled, lower = factor_and_route(
        chains, diag_block[0], mask, panel[0], contribution[0], pblk)
    return (lower[None], factor.reshape(1, rows, share), assembled.reshape(1, pblk * BS, share))


def from_root(value, axis, root):
    mine = lax.axis_index(axis) == root
    return lax.psum(jnp.where(mine, value, jnp.zeros_like(value)), axis)


def partner(value, axis, apart):
    mask = 2**apart
    pairs = [(source, source ^ mask) for source in range(lax.axis_size(axis))]
    return lax.ppermute(value, axis, pairs)


def on_large(diag_block, panel, pattern, contribution, route, slot):
    highest = lax.Precision.HIGHEST
    contract = (((1,), (1,)), ((), ()))
    whole = lax.all_gather(diag_block, ("row", "col"), axis=1, tiled=True)[0]
    width = whole.shape[0]
    lower = jnp.linalg.cholesky(whole)
    inverse = jax.scipy.linalg.solve_triangular(
        lower, jnp.eye(width, dtype=jnp.float32), lower=True
    )
    ncol = lax.axis_size("col")
    nrow = lax.axis_size("row")
    col_index = lax.axis_index("col")
    tile_mask = jnp.repeat(jnp.repeat(pattern[0], BS, axis=0), BS, axis=1).astype(jnp.float32)
    masked = panel[0] * tile_mask
    rows_dev = masked.shape[0]
    full_rows = lax.all_gather(masked, "col", axis=1, tiled=True)
    factor_rows = lax.dot_general(full_rows, inverse, contract, precision=highest)
    share = width // ncol
    own_cols = lax.dynamic_slice_in_dim(factor_rows, col_index * share, share, 1)
    cw_dev = contribution.shape[2]
    head_piece = lax.dynamic_slice_in_dim(factor_rows, col_index * cw_dev, cw_dev, 0)
    head_rows = from_root(head_piece, "row", 0)
    update = contribution[0] - lax.dot_general(factor_rows, head_rows, contract, precision=highest)
    blk = rows_dev // BS
    cap = max(2, blk // nrow)
    pblk = blk // 2
    blocks = update.reshape(blk, BS * cw_dev)
    target = route[0, :, 0]
    place = slot[0]
    order_ids = jnp.arange(blk, dtype=jnp.int32)
    earlier = (target[None, :] == target[:, None]) & (order_ids[None, :] < order_ids[:, None])
    rank = jnp.sum(earlier.astype(jnp.int32), axis=1)
    half = target // nrow
    target_row = target % nrow
    position = target_row * (2 * cap) + half * cap + rank
    slots_all = jnp.arange(nrow * 2 * cap, dtype=jnp.int32)
    onehot = (position[None, :] == slots_all[:, None]).astype(jnp.float32)
    packed = jnp.dot(onehot, blocks, precision=highest).reshape(nrow, 2, cap, BS * cw_dev)
    labels = jnp.dot(onehot, (place + 1).astype(jnp.float32), precision=highest).reshape(
        nrow, 2, cap
    )
    mine = lax.axis_index("cube") % 2
    got, got_labels = (
        lax.all_to_all(packed, "row", split_axis=0, concat_axis=0, tiled=True),
        lax.all_to_all(labels, "row", split_axis=0, concat_axis=0, tiled=True),
    )
    keep = lax.dynamic_index_in_dim(got, mine, 1, keepdims=False)
    keep_labels = lax.dynamic_index_in_dim(got_labels, mine, 1, keepdims=False)
    other = lax.dynamic_index_in_dim(got, 1 - mine, 1, keepdims=False)
    other_labels = lax.dynamic_index_in_dim(got_labels, 1 - mine, 1, keepdims=False)
    back, back_labels = partner((other, other_labels), "cube", 0)
    incoming = jnp.concatenate([keep, back], axis=0).reshape(-1, BS * cw_dev)
    tags = jnp.concatenate([keep_labels, back_labels], axis=0).reshape(-1)
    wanted = jnp.arange(1, pblk + 1, dtype=jnp.float32)
    select = (tags[None, :] == wanted[:, None]).astype(jnp.float32)
    assembled = jnp.dot(select, incoming, precision=highest).reshape(pblk * BS, cw_dev)
    rows_here = diag_block.shape[1]
    diag_rows = lax.dynamic_slice_in_dim(
        lower, lax.axis_index(("row", "col")) * rows_here, rows_here, 0
    )
    return (diag_rows[None], own_cols[None], assembled[None])


def solution(mesh):
    small = mesh.shape["row"] == 2 and mesh.shape["col"] == 4
    return jax.shard_map(
        on_small if small else on_large,
        mesh=mesh,
        in_specs=(
            P("cube", ("row", "col"), None),
            P("cube", "row", "col"),
            P("cube", "row", "col"),
            P("cube", "row", "col"),
            P("cube", "row", None),
            P("cube", "row"),
        ),
        out_specs=(
            P("cube", ("row", "col"), None),
            P("cube", "row", "col"),
            P("cube", "row", "col"),
        ),
        check_vma=False,
    )
```

```python
import functools

import jax
import jax.numpy as jnp
from jax import lax
from jax.experimental import pallas as pl
from jax.experimental.pallas import tpu as pltpu
from jax.sharding import PartitionSpec as P

BS = 128
HIGHEST = lax.Precision.HIGHEST
NT = (((1,), (1,)), ((), ()))
TN = (((0,), (0,)), ((), ()))
ANY = pl.BlockSpec(memory_space=pl.ANY)
VMEM = pl.BlockSpec(memory_space=pltpu.VMEM)
MESH = pl.DeviceIdType.MESH


def remote(src, dst, send, recv, device):
    return pltpu.make_async_remote_copy(
        src_ref=src, dst_ref=dst, send_sem=send, recv_sem=recv,
        device_id=device, device_id_type=MESH,
    )


def column(s, j):
    return jnp.take_along_axis(s, jnp.full(s.shape, j, jnp.int32), axis=1)


def factor_block(s_ref, x_ref, middle):
    n, w = BS, 8
    s = s_ref[...]
    for k in range(n // w):
        if k == n // w // 2:
            middle()
        o = w * k
        row = lax.broadcasted_iota(jnp.int32, (w, n), 0)
        lane = lax.broadcasted_iota(jnp.int32, (w, n), 1)
        full, rest = s[:w], s[w:]
        ct = [column(full, o + q) for q in range(w)]
        top = jnp.where((lane >= o) & (lane < o + w), (lane - o == row).astype(jnp.float32), full)
        more = o + w < n
        if more:
            cr = [column(rest, o + q) for q in range(w)]
            lanes = lax.broadcasted_iota(jnp.int32, rest.shape, 1)
            rest = jnp.where((lanes >= o) & (lanes < o + w), 0.0, rest)
        for t in range(0, w, 2):
            c0, c1 = ct[t], ct[t + 1]
            a, b, d = c0[t:t + 1], c1[t:t + 1], c1[t + 1:t + 2]
            inv = 1.0 / (a * d - b * b)
            below = row > t + 1
            m0 = jnp.where(below, (c0 * d - c1 * b) * inv, jnp.where(row == t + 1, b / a, 0.0))
            m1 = jnp.where(below, (c1 * a - c0 * b) * inv, 0.0)
            pairs = [(ct[q][t:t + 1], ct[q][t + 1:t + 2]) for q in range(w)]
            u0, u1 = top[t:t + 1], top[t + 1:t + 2]
            for q in range(t + 2, w):
                ct[q] = ct[q] - (m0 * pairs[q][0] + m1 * pairs[q][1])
            full = full - (m0 * full[t:t + 1] + m1 * full[t + 1:t + 2])
            top = top - (m0 * u0 + m1 * u1)
            if more:
                ai, bi, di = a * inv, b * inv, d * inv
                r0 = cr[t] * di - cr[t + 1] * bi
                r1 = cr[t + 1] * ai - cr[t] * bi
                for q in range(t + 2, w):
                    cr[q] = cr[q] - (r0 * pairs[q][0] + r1 * pairs[q][1])
                rest = rest - (r0 * u0 + r1 * u1)
        s_ref[o:o + w, :] = full
        x_ref[o:o + w, :] = jnp.where(lane <= row + o, top, 0.0)
        s = rest


def cholesky_inverse(a_ref, inv_ref, s_ref, x_ref, r_ref, middle, ready, between):
    width = a_ref.shape[0]
    sub = lax.broadcasted_iota(jnp.int32, (BS, BS), 0)
    lane = lax.broadcasted_iota(jnp.int32, (BS, BS), 1)
    inv_ref[...] = jnp.zeros_like(inv_ref)
    for p in range(width // BS):
        o, e = p * BS, (p + 1) * BS
        if p == 0:
            s_ref[...] = a_ref[o:e, o:e]
        else:
            left = a_ref[:o, o:e]
            s_ref[...] = a_ref[o:e, o:e] - lax.dot_general(left, left, TN, precision=HIGHEST)
            r_ref[:, :o] = -lax.dot_general(left, inv_ref[:o, :o], TN, precision=HIGHEST)
            if e < width:
                r_ref[:, e:] = a_ref[o:e, e:] - lax.dot_general(left, a_ref[:o, e:], TN, precision=HIGHEST)
        factor_block(s_ref, x_ref, middle if p == 0 else (lambda: None))
        if p == 0:
            ready()
        s = s_ref[...]
        d = jnp.sum(jnp.where(lane == sub, s, 0.0), axis=1, keepdims=True)
        rs = 1.0 / jnp.sqrt(d)
        x = x_ref[...] * rs
        a_ref[o:e, o:e] = jnp.where(lane >= sub, s, 0.0) * rs
        inv_ref[o:e, o:e] = x
        if p == 0:
            r_ref[:, e:] = a_ref[o:e, e:]
        if e < width:
            a_ref[o:e, e:] = jnp.dot(x, r_ref[:, e:], precision=HIGHEST)
        if p > 0:
            inv_ref[o:e, :o] = jnp.dot(x, r_ref[:, :o], precision=HIGHEST)
        between(p)


def to_column(row):
    n = row.shape[1]
    sub = lax.broadcasted_iota(jnp.int32, (n, n), 0)
    lane = lax.broadcasted_iota(jnp.int32, (n, n), 1)
    return jnp.sum(jnp.where(sub == lane, row, 0.0), axis=1, keepdims=True)


def chains(goal, slots, table_ref):
    n = goal.shape[1]
    sub = lax.broadcasted_iota(jnp.int32, (n, n), 0)
    lane = lax.broadcasted_iota(jnp.int32, (n, n), 1)
    goal_column = to_column(goal)
    earlier = (goal_column == goal) & (sub < lane)
    number = (sub + 1).astype(jnp.float32)
    prev = jnp.max(jnp.where(earlier, number, 0.0), axis=0, keepdims=True)
    names = lax.broadcasted_iota(jnp.int32, (n, slots), 1).astype(jnp.float32)
    number = (lax.broadcasted_iota(jnp.int32, (n, slots), 0) + 1).astype(jnp.float32)
    last = jnp.max(jnp.where(goal_column == names, number, 0.0), axis=0, keepdims=True)
    table_ref[...] = jnp.zeros_like(table_ref)
    table_ref[0:1, 0:n] = prev.astype(jnp.int32)
    table_ref[1:2, 0:slots] = last.astype(jnp.int32)


def gather_kernel(rows, route_ref, slot_ref, pattern_ref, diag_ref, panel_ref, contribution_ref,
                  f_ref, out_ref, l_ref,
                  own, g0, g1, g2, contrib, a_ref, inv_ref, s_ref, x_ref, r_ref, h_ref, hc_ref, v_ref,
                  vh_ref, vl_ref, masks, head_masks, pats, head_pats, pattern, route, slot, table, names, upd, t_ref, ra, rb, ra2, rb2,
                  dsend, drecv, xsend, xrecv, fsend, frecv, psend, precv, hsend, hrecv,
                  msend, mrecv, isem, asend, arecv, bsend, brecv, lsend, lrecv):
    z = lax.axis_index("cube")
    m = z % 2
    r, c = lax.axis_index("row"), lax.axis_index("col")
    y = 1 - r
    c1 = c + 1 - 2 * (c % 2)
    c2 = (c + 2) % 4
    c3 = (c1 + 2) % 4
    order = (c, c1, c2, c3)
    pieces = (own, g0, g1, g2)
    ndiag, width = diag_ref.shape
    blocks = panel_ref.shape[0]
    slices = BS // rows
    slots = out_ref.shape[0]
    half = slots // 2
    heads = width // BS
    to_x, to_core, to_row = {"col": c2}, {"col": c1}, {"row": y}
    to_cube = {"cube": z + 1 - 2 * m}

    def spot(rr, cc, k):
        return (pl.ds(pl.multiple_of((rr * 4 + cc) * ndiag, ndiag), ndiag),
                pl.ds(0, BS) if k == 0 else pl.ds(BS, width - BS))

    load_own = pltpu.make_async_copy(panel_ref, own, isem.at[0])
    load_contrib = pltpu.make_async_copy(contribution_ref, contrib, isem.at[1])
    load_diag = [pltpu.make_async_copy(
        diag_ref.at[:, spot(r, c, k)[1]], a_ref.at[spot(r, c, k)], isem.at[2 + k]) for k in range(2)]
    load_table = pltpu.make_async_copy(table, names, isem.at[4])
    load_small = [pltpu.make_async_copy(source, target, isem.at[5 + k]) for k, (source, target) in enumerate(
        ((pattern_ref, pattern), (route_ref, route), (slot_ref, slot)))]
    for copy in load_small + load_diag:
        copy.start()
    pats[...] = jnp.zeros_like(pats)
    barrier = pltpu.get_barrier_semaphore()
    for device in (to_x, to_core, to_row, to_cube):
        pl.semaphore_signal(barrier, inc=1, device_id=device, device_id_type=MESH)
    for copy in load_small:
        copy.wait()
    pats[0, 0:1, 0:blocks] = pattern[...].astype(jnp.float32)
    pl.semaphore_wait(barrier, 4)

    def spread(source, target):
        for j in range(4):
            target[j] = jnp.broadcast_to(to_column(source[j, 0:1, 0:blocks]), target.shape[1:])


    def piece_copy(k, n, rr, cc, device):
        part = spot(rr, cc, k)
        return remote(a_ref.at[part], a_ref.at[part], dsend.at[k, n], drecv.at[k, n], device)

    def own_copy(k, n, device):
        part = spot(r, c, k)
        return remote(diag_ref.at[:, part[1]], a_ref.at[part], dsend.at[k, n], drecv.at[k, n], device)

    diag = [(own_copy(k, 0, to_x), own_copy(k, 1, to_row), piece_copy(k, 2, r, c2, to_row),
             own_copy(k, 3, to_core), piece_copy(k, 4, r, c2, to_core), piece_copy(k, 5, y, c, to_core),
             piece_copy(k, 6, y, c2, to_core)) for k in range(2)]

    def sliced(i):
        return (pl.ds(heads, blocks - heads), pl.ds(pl.multiple_of(i * rows, rows), rows))

    top = (pl.ds(0, heads),)

    def across(i, part):
        return remote(panel_ref.at[part], g1.at[part], xsend.at[i], xrecv.at[i], to_x)

    def onward(i, part):
        return remote(g1.at[part], g2.at[part], fsend.at[i], frecv.at[i], to_core)

    def beside(i, part):
        return remote(panel_ref.at[part], g0.at[part], psend.at[i], precv.at[i], to_core)

    mask_x = remote(pats.at[0], pats.at[2], msend.at[0], mrecv.at[0], to_x)
    mask_core = remote(pats.at[0], pats.at[1], msend.at[1], mrecv.at[1], to_core)
    mask_on = remote(pats.at[2], pats.at[3], msend.at[2], mrecv.at[2], to_core)

    for k in range(2):
        for n in (0, 1, 3):
            diag[k][n].start()
    mask_x.start()
    across(slices, top).start()
    for i in range(slices):
        across(i, sliced(i)).start()
    mask_core.start()
    beside(slices, top).start()
    load_own.start()
    load_contrib.start()
    for k in range(2):
        diag[k][0].wait_recv()
        diag[k][2].start()
        diag[k][4].start()
        diag[k][1].wait_recv()
        diag[k][5].start()
        if k == 0:
            diag[k][2].wait_recv()
            diag[k][6].start()
            for n in (3, 4, 5, 6):
                diag[k][n].wait_recv()
    for copy in load_diag:
        copy.wait()

    def middle():
        diag[1][2].wait_recv()
        diag[1][6].start()

    def ready():
        for n in (3, 4, 5, 6):
            diag[1][n].wait_recv()
        for copies in diag:
            for copy in copies:
                copy.wait_send()

    head = [remote(piece.at[c], h_ref.at[j], hsend.at[j], hrecv.at[j], to_row) for j, piece in enumerate(pieces)]
    head_mask = remote(pats, head_pats, hsend.at[4], hrecv.at[4], to_row)

    def project(p):
        o, e = p * BS, (p + 1) * BS
        line = inv_ref[o:e, :e]
        part = lax.dot_general(line, hc_ref[:, :e], NT, precision=HIGHEST)
        term = lax.dot_general(line, part, TN, precision=HIGHEST)
        if o:
            v_ref[:o] = v_ref[:o] + term[:o]
        v_ref[o:e] = term[o:]

    def between(p):
        if p == 0:
            across(slices, top).wait_recv()
            onward(slices, top).start()
            mask_x.wait_recv()
            mask_on.start()
            for i in range(slices):
                beside(i, sliced(i)).start()
            chains((route[...] * slots + slot[...]).astype(jnp.float32), 4 * slots, table)
            load_table.start()
        if p == 1:
            load_own.wait()
            load_contrib.wait()
            beside(slices, top).wait_recv()
            onward(slices, top).wait_recv()
            mask_core.wait_recv()
            mask_on.wait_recv()
            spread(pats, masks)

            @pl.when(r == 0)
            def _():
                for copy in head:
                    copy.start()
                head_mask.start()
                for j, k in enumerate(order):
                    hc_ref[:, pl.ds(pl.multiple_of(k * BS, BS), BS)] = pieces[j][c] * masks[j, pl.ds(c, 1), :]

        if p == 2:
            @pl.when(r == 1)
            def _():
                for copy in head:
                    copy.wait_recv()
                head_mask.wait_recv()
                spread(head_pats, head_masks)
                for j, k in enumerate(order):
                    hc_ref[:, pl.ds(pl.multiple_of(k * BS, BS), BS)] = h_ref[j] * head_masks[j, pl.ds(c, 1), :]

            for q in range(3):
                project(q)
        if p == 3:
            project(3)

    cholesky_inverse(a_ref, inv_ref, s_ref, x_ref, r_ref, middle, ready, between)
    for j, k in enumerate(order):
        at = pl.ds(pl.multiple_of(k * BS, BS), BS)
        side = jnp.transpose(inv_ref[pl.ds(pl.multiple_of(c * BS, BS), BS), at])
        for q, value in ((0, side), (BS, v_ref[at, :])):
            high, low = split(value)
            vh_ref[j * BS:(j + 1) * BS, q:q + BS] = high
            vl_ref[j * BS:(j + 1) * BS, q:q + BS] = low

    def lower_rows():
        p = 2 * r + c // 2
        for k in range(heads):
            block = jnp.transpose(a_ref[k * BS:(k + 1) * BS, pl.ds(pl.multiple_of(p * BS, BS), BS)])
            s_ref[...] = jnp.where(k <= p, block, 0.0)
            l_ref[:, k * BS:(k + 1) * BS] = s_ref[pl.ds(pl.multiple_of((c % 2) * ndiag, ndiag), ndiag), :]

    load_table.wait()
    group = min(blocks, 512 // rows)

    def compute(i):
        part = pl.ds(pl.multiple_of(i * rows, rows), rows)

        def tile(q, carry):
            lines = []
            for b in range(group):
                at = q * group + b
                lines.append(jnp.concatenate(
                    [piece[at, part] * masks[j, pl.ds(at, 1), :] for j, piece in enumerate(pieces)], axis=1))
            high, low = split(jnp.concatenate(lines, axis=0))
            dot = functools.partial(jnp.dot, preferred_element_type=jnp.float32)
            out = dot(high, vh_ref[...]) + (dot(high, vl_ref[...]) + dot(low, vh_ref[...]))
            for b in range(group):
                at = q * group + b
                f_ref[at, part] = out[b * rows:(b + 1) * rows, :BS]
                update = contrib[at, part] - out[b * rows:(b + 1) * rows, BS:]
                name = names[0, at]
                upd[at] = update + jnp.where(name > 0, 1.0, 0.0) * upd[jnp.clip(name - 1, 0, blocks - 1)]
            return carry

        lax.fori_loop(0, blocks // group, tile, 0)

        def fill(q, carry):
            for b in range(16):
                k = q * 16 + b
                name = names[1, k]
                t_ref[i, k] = upd[jnp.clip(name - 1, 0, blocks - 1)] * jnp.where(name > 0, 1.0, 0.0)
            return carry

        lax.fori_loop(0, 4 * slots // 16, fill, 0)

    def quarter(g, low):
        return pl.ds(g * slots + (0 if low else half), half)

    def hops(i):
        goal = ((1 - m) * 2 + y, m * 2 + y, (1 - m) * 2 + r)
        over_a = [remote(t_ref.at[i, quarter(goal[k], True)], ra.at[k, i],
                         asend.at[k, i], arecv.at[k, i], to_row) for k in range(2)]
        over_b = [remote(t_ref.at[i, quarter(goal[2 * k], False)], rb.at[k, i],
                         bsend.at[k, i], brecv.at[k, i], to_cube) for k in range(2)]
        last = [remote(ra.at[0, i], ra2.at[i], lsend.at[0, i], lrecv.at[0, i], to_cube),
                remote(rb.at[0, i], rb2.at[i], lsend.at[1, i], lrecv.at[1, i], to_row)]
        return over_a, over_b, last

    def turn(i):
        over_a, over_b, last = hops(i)
        over_a[0].wait_recv()
        ra[0, i] = ra[0, i] + t_ref[i, quarter((1 - m) * 2 + r, True)]
        last[0].start()
        over_b[0].wait_recv()
        rb[0, i] = rb[0, i] + t_ref[i, quarter(m * 2 + y, False)]
        last[1].start()

    def finish(i):
        part = pl.ds(pl.multiple_of(i * rows, rows), rows)
        over_a, over_b, last = hops(i)
        over_a[1].wait_recv()
        last[0].wait_recv()
        out_ref[pl.ds(0, half), part] = t_ref[i, quarter(m * 2 + r, True)] + ra[1, i] + ra2[i]
        over_b[1].wait_recv()
        last[1].wait_recv()
        out_ref[pl.ds(half, half), part] = t_ref[i, quarter(m * 2 + r, False)] + rb[1, i] + rb2[i]

    upd[...] = jnp.zeros_like(upd)

    def step(i, carry):
        @pl.when(i == 3)
        def _():
            lower_rows()

        @pl.when(i < slices)
        def _():
            across(i, sliced(i)).wait_recv()
            onward(i, sliced(i)).start()

        @pl.when(i == slices - 1)
        def _():
            turn(i - 1)

        @pl.when(i < slices)
        def _():
            beside(i, sliced(i)).wait_recv()
            onward(i, sliced(i)).wait_recv()
            compute(i)
            over_a, over_b, _ = hops(i)
            for k in range(2):
                over_a[k].start()
                over_b[k].start()

        @pl.when((i > 0) & (i <= slices) & (i != slices - 1))
        def _():
            turn(i - 1)

        @pl.when(i > 2)
        def _():
            finish(i - 3)

        @pl.when(i > 3)
        def _():
            drain(i - 4)
        return carry

    def drain(i):
        over_a, over_b, last = hops(i)
        for copy in over_a + over_b + last + [across(i, sliced(i)), onward(i, sliced(i)), beside(i, sliced(i))]:
            copy.wait_send()

    lax.fori_loop(0, slices + 3, step, 0)

    for i in (slices - 1,):
        drain(i)
    for copy in (across(slices, top), onward(slices, top), beside(slices, top), mask_x, mask_core, mask_on):
        copy.wait_send()

    @pl.when(r == 0)
    def _():
        for copy in head:
            copy.wait_send()
        head_mask.wait_send()


def factor_and_route(route, slot, pattern, diag, panel, contribution):
    rows = 8
    slices = BS // rows
    tall, share = panel.shape
    blk = tall // BS
    pblk = blk // 2
    half = pblk // 2
    ndiag, width = diag.shape
    whole = pltpu.VMEM((blk, BS, share), jnp.float32)
    square = pltpu.VMEM((width, width), jnp.float32)
    block = pltpu.VMEM((BS, BS), jnp.float32)
    sems = pltpu.SemaphoreType.DMA
    return pl.pallas_call(
        functools.partial(gather_kernel, rows),
        out_shape=(
            pltpu.VMEM((blk, BS, share), jnp.float32),
            pltpu.VMEM((pblk, BS, share), jnp.float32),
            pltpu.VMEM((ndiag, width), jnp.float32),
        ),
        in_specs=[ANY] * 6,
        out_specs=(VMEM, VMEM, VMEM),
        scratch_shapes=[
            whole, whole, whole, whole, whole,
            square, square, block, block,
            pltpu.VMEM((BS, width), jnp.float32),
            pltpu.VMEM((4, BS, BS), jnp.float32),
            pltpu.VMEM((BS, width), jnp.float32),
            pltpu.VMEM((width, BS), jnp.float32),
            pltpu.VMEM((width, 2 * BS), jnp.bfloat16),
            pltpu.VMEM((width, 2 * BS), jnp.bfloat16),
            pltpu.VMEM((4, blk, share), jnp.float32),
            pltpu.VMEM((4, blk, share), jnp.float32),
            pltpu.VMEM((4, 8, BS), jnp.float32),
            pltpu.VMEM((4, 8, BS), jnp.float32),
            pltpu.VMEM((1, blk), jnp.int32),
            pltpu.VMEM((1, blk), jnp.int32),
            pltpu.VMEM((1, blk), jnp.int32),
            pltpu.VMEM((8, BS), jnp.int32),
            pltpu.SMEM((8, BS), jnp.int32),
            pltpu.VMEM((blk, rows, share), jnp.float32),
            pltpu.VMEM((slices, 4 * pblk, rows, share), jnp.float32),
            pltpu.VMEM((2, slices, half, rows, share), jnp.float32),
            pltpu.VMEM((2, slices, half, rows, share), jnp.float32),
            pltpu.VMEM((slices, half, rows, share), jnp.float32),
            pltpu.VMEM((slices, half, rows, share), jnp.float32),
            sems((2, 7)), sems((2, 7)),
            sems((slices + 1,)), sems((slices + 1,)), sems((slices + 1,)), sems((slices + 1,)),
            sems((slices + 1,)), sems((slices + 1,)), sems((5,)), sems((5,)), sems((3,)), sems((3,)),
            sems((8,)),
            sems((2, slices)), sems((2, slices)), sems((2, slices)), sems((2, slices)),
            sems((2, slices)), sems((2, slices)),
        ],
        compiler_params=pltpu.CompilerParams(
            collective_id=0, has_side_effects=True, vmem_limit_bytes=48 * 2**20),
        name="gather_factor",
    )(route, slot, pattern, diag, panel.reshape(blk, BS, share), contribution.reshape(blk, BS, share))


def split(value):
    high = value.astype(jnp.bfloat16)
    return high, (value - high.astype(jnp.float32)).astype(jnp.bfloat16)


def on_small(diag_block, panel, pattern, contribution, route, slot):
    rows, share = panel.shape[1:]
    blk = rows // BS
    factor, assembled, lower = factor_and_route(
        route.reshape(1, blk), slot.reshape(1, blk), pattern.reshape(1, blk),
        diag_block[0], panel[0], contribution[0])
    return (lower[None], factor.reshape(1, rows, share), assembled.reshape(1, rows // 2, share))


def from_root(value, axis, root):
    mine = lax.axis_index(axis) == root
    return lax.psum(jnp.where(mine, value, jnp.zeros_like(value)), axis)


def partner(value, axis, apart):
    mask = 2**apart
    pairs = [(source, source ^ mask) for source in range(lax.axis_size(axis))]
    return lax.ppermute(value, axis, pairs)


def on_large(diag_block, panel, pattern, contribution, route, slot):
    highest = lax.Precision.HIGHEST
    contract = (((1,), (1,)), ((), ()))
    whole = lax.all_gather(diag_block, ("row", "col"), axis=1, tiled=True)[0]
    width = whole.shape[0]
    lower = jnp.linalg.cholesky(whole)
    inverse = jax.scipy.linalg.solve_triangular(
        lower, jnp.eye(width, dtype=jnp.float32), lower=True
    )
    ncol = lax.axis_size("col")
    nrow = lax.axis_size("row")
    col_index = lax.axis_index("col")
    tile_mask = jnp.repeat(jnp.repeat(pattern[0], BS, axis=0), BS, axis=1).astype(jnp.float32)
    masked = panel[0] * tile_mask
    rows_dev = masked.shape[0]
    full_rows = lax.all_gather(masked, "col", axis=1, tiled=True)
    factor_rows = lax.dot_general(full_rows, inverse, contract, precision=highest)
    share = width // ncol
    own_cols = lax.dynamic_slice_in_dim(factor_rows, col_index * share, share, 1)
    cw_dev = contribution.shape[2]
    head_piece = lax.dynamic_slice_in_dim(factor_rows, col_index * cw_dev, cw_dev, 0)
    head_rows = from_root(head_piece, "row", 0)
    update = contribution[0] - lax.dot_general(factor_rows, head_rows, contract, precision=highest)
    blk = rows_dev // BS
    cap = max(2, blk // nrow)
    pblk = blk // 2
    blocks = update.reshape(blk, BS * cw_dev)
    target = route[0, :, 0]
    place = slot[0]
    order_ids = jnp.arange(blk, dtype=jnp.int32)
    earlier = (target[None, :] == target[:, None]) & (order_ids[None, :] < order_ids[:, None])
    rank = jnp.sum(earlier.astype(jnp.int32), axis=1)
    half = target // nrow
    target_row = target % nrow
    position = target_row * (2 * cap) + half * cap + rank
    slots_all = jnp.arange(nrow * 2 * cap, dtype=jnp.int32)
    onehot = (position[None, :] == slots_all[:, None]).astype(jnp.float32)
    packed = jnp.dot(onehot, blocks, precision=highest).reshape(nrow, 2, cap, BS * cw_dev)
    labels = jnp.dot(onehot, (place + 1).astype(jnp.float32), precision=highest).reshape(
        nrow, 2, cap
    )
    mine = lax.axis_index("cube") % 2
    got, got_labels = (
        lax.all_to_all(packed, "row", split_axis=0, concat_axis=0, tiled=True),
        lax.all_to_all(labels, "row", split_axis=0, concat_axis=0, tiled=True),
    )
    keep = lax.dynamic_index_in_dim(got, mine, 1, keepdims=False)
    keep_labels = lax.dynamic_index_in_dim(got_labels, mine, 1, keepdims=False)
    other = lax.dynamic_index_in_dim(got, 1 - mine, 1, keepdims=False)
    other_labels = lax.dynamic_index_in_dim(got_labels, 1 - mine, 1, keepdims=False)
    back, back_labels = partner((other, other_labels), "cube", 0)
    incoming = jnp.concatenate([keep, back], axis=0).reshape(-1, BS * cw_dev)
    tags = jnp.concatenate([keep_labels, back_labels], axis=0).reshape(-1)
    wanted = jnp.arange(1, pblk + 1, dtype=jnp.float32)
    select = (tags[None, :] == wanted[:, None]).astype(jnp.float32)
    assembled = jnp.dot(select, incoming, precision=highest).reshape(pblk * BS, cw_dev)
    rows_here = diag_block.shape[1]
    diag_rows = lax.dynamic_slice_in_dim(
        lower, lax.axis_index(("row", "col")) * rows_here, rows_here, 0
    )
    return (diag_rows[None], own_cols[None], assembled[None])


def solution(mesh):
    small = mesh.shape["row"] == 2 and mesh.shape["col"] == 4
    return jax.shard_map(
        on_small if small else on_large,
        mesh=mesh,
        in_specs=(
            P("cube", ("row", "col"), None),
            P("cube", "row", "col"),
            P("cube", "row", "col"),
            P("cube", "row", "col"),
            P("cube", "row", None),
            P("cube", "row"),
        ),
        out_specs=(
            P("cube", ("row", "col"), None),
            P("cube", "row", "col"),
            P("cube", "row", "col"),
        ),
        check_vma=False,
    )
```

```python
import functools

import jax
import jax.numpy as jnp
from jax import lax
from jax.experimental import pallas as pl
from jax.experimental.pallas import tpu as pltpu
from jax.sharding import PartitionSpec as P

BS = 128
HIGHEST = lax.Precision.HIGHEST
NT = (((1,), (1,)), ((), ()))
TN = (((0,), (0,)), ((), ()))
ANY = pl.BlockSpec(memory_space=pl.ANY)
VMEM = pl.BlockSpec(memory_space=pltpu.VMEM)
MESH = pl.DeviceIdType.MESH


def remote(src, dst, send, recv, device):
    return pltpu.make_async_remote_copy(
        src_ref=src, dst_ref=dst, send_sem=send, recv_sem=recv,
        device_id=device, device_id_type=MESH,
    )


def column(s, j):
    return jnp.take_along_axis(s, jnp.full(s.shape, j, jnp.int32), axis=1)


def factor_block(s_ref, x_ref, middle):
    n, w = BS, 8
    s = s_ref[...]
    for k in range(n // w):
        if k == n // w // 2:
            middle()
        o = w * k
        row = lax.broadcasted_iota(jnp.int32, (w, n), 0)
        lane = lax.broadcasted_iota(jnp.int32, (w, n), 1)
        full, rest = s[:w], s[w:]
        ct = [column(full, o + q) for q in range(w)]
        top = jnp.where((lane >= o) & (lane < o + w), (lane - o == row).astype(jnp.float32), full)
        more = o + w < n
        if more:
            cr = [column(rest, o + q) for q in range(w)]
            lanes = lax.broadcasted_iota(jnp.int32, rest.shape, 1)
            rest = jnp.where((lanes >= o) & (lanes < o + w), 0.0, rest)
        for t in range(0, w, 2):
            c0, c1 = ct[t], ct[t + 1]
            a, b, d = c0[t:t + 1], c1[t:t + 1], c1[t + 1:t + 2]
            inv = 1.0 / (a * d - b * b)
            below = row > t + 1
            m0 = jnp.where(below, (c0 * d - c1 * b) * inv, jnp.where(row == t + 1, b / a, 0.0))
            m1 = jnp.where(below, (c1 * a - c0 * b) * inv, 0.0)
            pairs = [(ct[q][t:t + 1], ct[q][t + 1:t + 2]) for q in range(w)]
            u0, u1 = top[t:t + 1], top[t + 1:t + 2]
            for q in range(t + 2, w):
                ct[q] = ct[q] - (m0 * pairs[q][0] + m1 * pairs[q][1])
            full = full - (m0 * full[t:t + 1] + m1 * full[t + 1:t + 2])
            top = top - (m0 * u0 + m1 * u1)
            if more:
                ai, bi, di = a * inv, b * inv, d * inv
                r0 = cr[t] * di - cr[t + 1] * bi
                r1 = cr[t + 1] * ai - cr[t] * bi
                for q in range(t + 2, w):
                    cr[q] = cr[q] - (r0 * pairs[q][0] + r1 * pairs[q][1])
                rest = rest - (r0 * u0 + r1 * u1)
        s_ref[o:o + w, :] = full
        x_ref[o:o + w, :] = jnp.where(lane <= row + o, top, 0.0)
        s = rest


def cholesky_inverse(a_ref, inv_ref, s_ref, x_ref, r_ref, middle, ready, between):
    width = a_ref.shape[0]
    sub = lax.broadcasted_iota(jnp.int32, (BS, BS), 0)
    lane = lax.broadcasted_iota(jnp.int32, (BS, BS), 1)
    inv_ref[...] = jnp.zeros_like(inv_ref)
    for p in range(width // BS):
        o, e = p * BS, (p + 1) * BS
        if p == 0:
            s_ref[...] = a_ref[o:e, o:e]
        else:
            left = a_ref[:o, o:e]
            s_ref[...] = a_ref[o:e, o:e] - lax.dot_general(left, left, TN, precision=HIGHEST)
            r_ref[:, :o] = -lax.dot_general(left, inv_ref[:o, :o], TN, precision=HIGHEST)
            if e < width:
                r_ref[:, e:] = a_ref[o:e, e:] - lax.dot_general(left, a_ref[:o, e:], TN, precision=HIGHEST)
        factor_block(s_ref, x_ref, middle if p == 0 else (lambda: None))
        if p == 0:
            ready()
        s = s_ref[...]
        d = jnp.sum(jnp.where(lane == sub, s, 0.0), axis=1, keepdims=True)
        rs = 1.0 / jnp.sqrt(d)
        x = x_ref[...] * rs
        a_ref[o:e, o:e] = jnp.where(lane >= sub, s, 0.0) * rs
        inv_ref[o:e, o:e] = x
        if p == 0:
            r_ref[:, e:] = a_ref[o:e, e:]
        if e < width:
            a_ref[o:e, e:] = jnp.dot(x, r_ref[:, e:], precision=HIGHEST)
        if p > 0:
            inv_ref[o:e, :o] = jnp.dot(x, r_ref[:, :o], precision=HIGHEST)
        between(p)


def to_column(row):
    n = row.shape[1]
    sub = lax.broadcasted_iota(jnp.int32, (n, n), 0)
    lane = lax.broadcasted_iota(jnp.int32, (n, n), 1)
    return jnp.sum(jnp.where(sub == lane, row, 0.0), axis=1, keepdims=True)


def chains(goal, slots, table_ref):
    n = goal.shape[1]
    sub = lax.broadcasted_iota(jnp.int32, (n, n), 0)
    lane = lax.broadcasted_iota(jnp.int32, (n, n), 1)
    goal_column = to_column(goal)
    earlier = (goal_column == goal) & (sub < lane)
    number = (sub + 1).astype(jnp.float32)
    prev = jnp.max(jnp.where(earlier, number, 0.0), axis=0, keepdims=True)
    names = lax.broadcasted_iota(jnp.int32, (n, slots), 1).astype(jnp.float32)
    number = (lax.broadcasted_iota(jnp.int32, (n, slots), 0) + 1).astype(jnp.float32)
    last = jnp.max(jnp.where(goal_column == names, number, 0.0), axis=0, keepdims=True)
    table_ref[...] = jnp.zeros_like(table_ref)
    table_ref[0:1, 0:n] = prev.astype(jnp.int32)
    table_ref[1:2, 0:slots] = last.astype(jnp.int32)


def gather_kernel(rows, route_ref, slot_ref, pattern_ref, diag_ref, panel_ref, contribution_ref,
                  f_ref, out_ref, l_ref,
                  own, g0, g1, g2, contrib, a_ref, inv_ref, s_ref, x_ref, r_ref, hh_ref, h_ref, hc_ref, v_ref,
                  vh_ref, vl_ref, masks, head_masks, pats, head_pats, pattern, route, slot, table, names, upd, t_ref, ra, rb, ra2, rb2,
                  dsend, drecv, xsend, xrecv, fsend, frecv, psend, precv, hsend, hrecv,
                  msend, mrecv, isem, asend, arecv, bsend, brecv, lsend, lrecv):
    z = lax.axis_index("cube")
    m = z % 2
    r, c = lax.axis_index("row"), lax.axis_index("col")
    y = 1 - r
    c1 = c + 1 - 2 * (c % 2)
    c2 = (c + 2) % 4
    c3 = (c1 + 2) % 4
    order = (c, c1, c2, c3)
    pieces = (own, g0, g1, g2)
    ndiag, width = diag_ref.shape
    blocks = panel_ref.shape[0]
    slices = BS // rows
    slots = out_ref.shape[0]
    half = slots // 2
    heads = width // BS
    to_x, to_core, to_row = {"col": c2}, {"col": c1}, {"row": y}
    to_cube = {"cube": z + 1 - 2 * m}

    def spot(rr, cc, k):
        return (pl.ds(pl.multiple_of((rr * 4 + cc) * ndiag, ndiag), ndiag),
                pl.ds(0, BS) if k == 0 else pl.ds(BS, width - BS))

    load_own = pltpu.make_async_copy(panel_ref, own, isem.at[0])
    load_contrib = pltpu.make_async_copy(contribution_ref, contrib, isem.at[1])
    load_diag = [pltpu.make_async_copy(
        diag_ref.at[:, spot(r, c, k)[1]], a_ref.at[spot(r, c, k)], isem.at[2 + k]) for k in range(2)]
    load_table = pltpu.make_async_copy(table, names, isem.at[4])
    load_small = [pltpu.make_async_copy(source, target, isem.at[5 + k]) for k, (source, target) in enumerate(
        ((pattern_ref, pattern), (route_ref, route), (slot_ref, slot)))]
    for copy in load_small + load_diag:
        copy.start()
    pats[...] = jnp.zeros_like(pats)
    barrier = pltpu.get_barrier_semaphore()
    for device in (to_x, to_core, to_row, to_cube):
        pl.semaphore_signal(barrier, inc=1, device_id=device, device_id_type=MESH)
    for copy in load_small:
        copy.wait()
    pats[0, 0:1, 0:blocks] = pattern[...].astype(jnp.float32)
    pl.semaphore_wait(barrier, 4)

    def spread(source, target):
        for j in range(4):
            target[j] = jnp.broadcast_to(to_column(source[j, 0:1, 0:blocks]), target.shape[1:])


    def even(rr, cc, k):
        return spot(rr, cc, k)[0], pl.ds(pl.multiple_of((cc // 2 + 2 * k) * BS, BS), BS)

    def piece_copy(k, n, part, device):
        return remote(a_ref.at[part], a_ref.at[part], dsend.at[k, n], drecv.at[k, n], device)

    def own_copy(k, n, part, device):
        return remote(diag_ref.at[:, part[1]], a_ref.at[part], dsend.at[k, n], drecv.at[k, n], device)

    diag = [(own_copy(k, 0, even(r, c, k), to_x), own_copy(k, 1, spot(r, c, k), to_row),
             piece_copy(k, 2, even(r, c2, k), to_row), own_copy(k, 3, spot(r, c, k), to_core),
             piece_copy(k, 4, even(r, c2, k), to_core), piece_copy(k, 5, spot(y, c, k), to_core),
             piece_copy(k, 6, even(y, c2, k), to_core)) for k in range(2)]

    def sliced(i):
        return (pl.ds(heads, blocks - heads), pl.ds(pl.multiple_of(i * rows, rows), rows))

    top = (pl.ds(0, heads),)

    def across(i, part):
        return remote(panel_ref.at[part], g1.at[part], xsend.at[i], xrecv.at[i], to_x)

    def onward(i, part):
        return remote(g1.at[part], g2.at[part], fsend.at[i], frecv.at[i], to_core)

    def beside(i, part):
        return remote(panel_ref.at[part], g0.at[part], psend.at[i], precv.at[i], to_core)

    pair = pl.ds(2 * (c // 2), 2)
    head = [remote(source.at[pair], hh_ref.at[k], hsend.at[k], hrecv.at[k], to_row)
            for k, source in enumerate((panel_ref, g1))]
    swap = [remote(hh_ref.at[k, 1 - c % 2], h_ref.at[k], hsend.at[2 + k], hrecv.at[2 + k], to_core) for k in range(2)]
    mask_x = remote(pats.at[0], pats.at[2], msend.at[0], mrecv.at[0], to_x)
    mask_core = remote(pats.at[0], pats.at[1], msend.at[1], mrecv.at[1], to_core)
    mask_on = remote(pats.at[2], pats.at[3], msend.at[2], mrecv.at[2], to_core)

    for k in range(2):
        for n in (0, 1, 3):
            diag[k][n].start()
    mask_x.start()

    @pl.when(r == 0)
    def _():
        head[0].start()

    across(slices, top).start()
    for i in range(slices):
        across(i, sliced(i)).start()
    mask_core.start()
    beside(slices, top).start()
    load_own.start()
    load_contrib.start()
    for k in range(2):
        diag[k][0].wait_recv()
        diag[k][2].start()
        diag[k][4].start()
        diag[k][1].wait_recv()
        diag[k][5].start()
        if k == 0:
            diag[k][2].wait_recv()
            diag[k][6].start()
            for n in (3, 4, 5, 6):
                diag[k][n].wait_recv()
    for copy in load_diag:
        copy.wait()

    def middle():
        diag[1][2].wait_recv()
        diag[1][6].start()

    def ready():
        for n in (3, 4, 5, 6):
            diag[1][n].wait_recv()
        for copies in diag:
            for copy in copies:
                copy.wait_send()

        def mirror(i, j):
            a_ref[i * BS:(i + 1) * BS, j * BS:(j + 1) * BS] = jnp.transpose(
                a_ref[j * BS:(j + 1) * BS, i * BS:(i + 1) * BS])

        for side in range(2):
            @pl.when(c // 2 == side)
            def _():
                for i in range(1 - side, heads, 2):
                    for j in range(i + 1, heads, 2):
                        mirror(i, j)

    head_mask = remote(pats, head_pats, hsend.at[4], hrecv.at[4], to_row)

    def project(p):
        o, e = p * BS, (p + 1) * BS
        line = inv_ref[o:e, :e]
        part = lax.dot_general(line, hc_ref[:, :e], NT, precision=HIGHEST)
        term = lax.dot_general(line, part, TN, precision=HIGHEST)
        if o:
            v_ref[:o] = v_ref[:o] + term[:o]
        v_ref[o:e] = term[o:]

    def between(p):
        if p == 0:
            across(slices, top).wait_recv()
            onward(slices, top).start()

            @pl.when(r == 0)
            def _():
                head[1].start()

            mask_x.wait_recv()
            mask_on.start()
            for i in range(slices):
                beside(i, sliced(i)).start()
            chains((route[...] * slots + slot[...]).astype(jnp.float32), 4 * slots, table)
            load_table.start()
        if p == 1:
            load_own.wait()
            load_contrib.wait()
            beside(slices, top).wait_recv()
            onward(slices, top).wait_recv()
            mask_core.wait_recv()
            mask_on.wait_recv()
            spread(pats, masks)

            @pl.when(r == 0)
            def _():
                head_mask.start()
                for j, k in enumerate(order):
                    hc_ref[:, pl.ds(pl.multiple_of(k * BS, BS), BS)] = pieces[j][c] * masks[j, pl.ds(c, 1), :]

            @pl.when(r == 1)
            def _():
                for k in range(2):
                    head[k].wait_recv()
                    swap[k].start()

        if p == 2:
            @pl.when(r == 1)
            def _():
                for copy in swap:
                    copy.wait_recv()
                head_mask.wait_recv()
                spread(head_pats, head_masks)
                heads_in = (hh_ref[0, c % 2], h_ref[0], hh_ref[1, c % 2], h_ref[1])
                for j, k in enumerate(order):
                    hc_ref[:, pl.ds(pl.multiple_of(k * BS, BS), BS)] = heads_in[j] * head_masks[j, pl.ds(c, 1), :]

            for q in range(3):
                project(q)
        if p == 3:
            project(3)

    cholesky_inverse(a_ref, inv_ref, s_ref, x_ref, r_ref, middle, ready, between)
    for j, k in enumerate(order):
        at = pl.ds(pl.multiple_of(k * BS, BS), BS)
        side = jnp.transpose(inv_ref[pl.ds(pl.multiple_of(c * BS, BS), BS), at])
        for q, value in ((0, side), (BS, v_ref[at, :])):
            high, low = split(value)
            vh_ref[j * BS:(j + 1) * BS, q:q + BS] = high
            vl_ref[j * BS:(j + 1) * BS, q:q + BS] = low

    def lower_rows():
        p = 2 * r + c // 2
        for k in range(heads):
            block = jnp.transpose(a_ref[k * BS:(k + 1) * BS, pl.ds(pl.multiple_of(p * BS, BS), BS)])
            s_ref[...] = jnp.where(k <= p, block, 0.0)
            l_ref[:, k * BS:(k + 1) * BS] = s_ref[pl.ds(pl.multiple_of((c % 2) * ndiag, ndiag), ndiag), :]

    load_table.wait()
    group = min(blocks, 512 // rows)

    def compute(i):
        part = pl.ds(pl.multiple_of(i * rows, rows), rows)

        def tile(q, carry):
            lines = []
            for b in range(group):
                at = q * group + b
                lines.append(jnp.concatenate(
                    [piece[at, part] * masks[j, pl.ds(at, 1), :] for j, piece in enumerate(pieces)], axis=1))
            high, low = split(jnp.concatenate(lines, axis=0))
            dot = functools.partial(jnp.dot, preferred_element_type=jnp.float32)
            out = dot(high, vh_ref[...]) + (dot(high, vl_ref[...]) + dot(low, vh_ref[...]))
            for b in range(group):
                at = q * group + b
                f_ref[at, part] = out[b * rows:(b + 1) * rows, :BS]
                update = contrib[at, part] - out[b * rows:(b + 1) * rows, BS:]
                name = names[0, at]
                upd[at] = update + jnp.where(name > 0, 1.0, 0.0) * upd[jnp.clip(name - 1, 0, blocks - 1)]
            return carry

        lax.fori_loop(0, blocks // group, tile, 0)

    def fill(i, start):
        def body(q, carry):
            for b in range(16):
                k = start + q * 16 + b
                name = names[1, k]
                t_ref[i, k] = upd[jnp.clip(name - 1, 0, blocks - 1)] * jnp.where(name > 0, 1.0, 0.0)
            return carry

        lax.fori_loop(0, half // 16, body, 0)

    def quarter(g, low):
        return pl.ds(g * slots + (0 if low else half), half)

    def hops(i):
        goal = ((1 - m) * 2 + y, m * 2 + y, (1 - m) * 2 + r)
        over_a = [remote(t_ref.at[i, quarter(goal[k], True)], ra.at[k, i],
                         asend.at[k, i], arecv.at[k, i], to_row) for k in range(2)]
        over_b = [remote(t_ref.at[i, quarter(goal[2 * k], False)], rb.at[k, i],
                         bsend.at[k, i], brecv.at[k, i], to_cube) for k in range(2)]
        last = [remote(ra.at[0, i], ra2.at[i], lsend.at[0, i], lrecv.at[0, i], to_cube),
                remote(rb.at[0, i], rb2.at[i], lsend.at[1, i], lrecv.at[1, i], to_row)]
        return over_a, over_b, last

    def turn(i):
        over_a, over_b, last = hops(i)
        over_a[0].wait_recv()
        ra[0, i] = ra[0, i] + t_ref[i, quarter((1 - m) * 2 + r, True)]
        last[0].start()
        over_b[0].wait_recv()
        rb[0, i] = rb[0, i] + t_ref[i, quarter(m * 2 + y, False)]
        last[1].start()

    def finish(i):
        part = pl.ds(pl.multiple_of(i * rows, rows), rows)
        over_a, over_b, last = hops(i)
        over_a[1].wait_recv()
        last[0].wait_recv()
        out_ref[pl.ds(0, half), part] = t_ref[i, quarter(m * 2 + r, True)] + ra[1, i] + ra2[i]
        over_b[1].wait_recv()
        last[1].wait_recv()
        out_ref[pl.ds(half, half), part] = t_ref[i, quarter(m * 2 + r, False)] + rb[1, i] + rb2[i]

    upd[...] = jnp.zeros_like(upd)

    def step(i, carry):
        @pl.when(i == 3)
        def _():
            lower_rows()

        @pl.when(i < slices)
        def _():
            across(i, sliced(i)).wait_recv()
            onward(i, sliced(i)).start()

        @pl.when(i == slices - 1)
        def _():
            turn(i - 1)

        @pl.when(i < slices)
        def _():
            beside(i, sliced(i)).wait_recv()
            onward(i, sliced(i)).wait_recv()
            compute(i)
            over_a, over_b, _ = hops(i)
            here, there, above = (m * 2 + y) * slots, ((1 - m) * 2 + y) * slots, ((1 - m) * 2 + r) * slots
            fill(i, there)
            over_a[0].start()
            fill(i, there + half)
            over_b[0].start()
            fill(i, here)
            over_a[1].start()
            fill(i, above + half)
            over_b[1].start()
            for start in (above, here + half, (m * 2 + r) * slots, (m * 2 + r) * slots + half):
                fill(i, start)

        @pl.when((i > 0) & (i <= slices) & (i != slices - 1))
        def _():
            turn(i - 1)

        @pl.when(i > 2)
        def _():
            finish(i - 3)

        @pl.when(i > 3)
        def _():
            drain(i - 4)
        return carry

    def drain(i):
        over_a, over_b, last = hops(i)
        for copy in over_a + over_b + last + [across(i, sliced(i)), onward(i, sliced(i)), beside(i, sliced(i))]:
            copy.wait_send()

    lax.fori_loop(0, slices + 3, step, 0)

    for i in (slices - 1,):
        drain(i)
    for copy in (across(slices, top), onward(slices, top), beside(slices, top), mask_x, mask_core, mask_on):
        copy.wait_send()

    @pl.when(r == 0)
    def _():
        for copy in head:
            copy.wait_send()
        head_mask.wait_send()

    @pl.when(r == 1)
    def _():
        for copy in swap:
            copy.wait_send()


def factor_and_route(route, slot, pattern, diag, panel, contribution):
    rows = 8
    slices = BS // rows
    tall, share = panel.shape
    blk = tall // BS
    pblk = blk // 2
    half = pblk // 2
    ndiag, width = diag.shape
    whole = pltpu.VMEM((blk, BS, share), jnp.float32)
    square = pltpu.VMEM((width, width), jnp.float32)
    block = pltpu.VMEM((BS, BS), jnp.float32)
    sems = pltpu.SemaphoreType.DMA
    return pl.pallas_call(
        functools.partial(gather_kernel, rows),
        out_shape=(
            pltpu.VMEM((blk, BS, share), jnp.float32),
            pltpu.VMEM((pblk, BS, share), jnp.float32),
            pltpu.VMEM((ndiag, width), jnp.float32),
        ),
        in_specs=[ANY] * 6,
        out_specs=(VMEM, VMEM, VMEM),
        scratch_shapes=[
            whole, whole, whole, whole, whole,
            square, square, block, block,
            pltpu.VMEM((BS, width), jnp.float32),
            pltpu.VMEM((2, 2, BS, BS), jnp.float32),
            pltpu.VMEM((2, BS, BS), jnp.float32),
            pltpu.VMEM((BS, width), jnp.float32),
            pltpu.VMEM((width, BS), jnp.float32),
            pltpu.VMEM((width, 2 * BS), jnp.bfloat16),
            pltpu.VMEM((width, 2 * BS), jnp.bfloat16),
            pltpu.VMEM((4, blk, share), jnp.float32),
            pltpu.VMEM((4, blk, share), jnp.float32),
            pltpu.VMEM((4, 8, BS), jnp.float32),
            pltpu.VMEM((4, 8, BS), jnp.float32),
            pltpu.VMEM((1, blk), jnp.int32),
            pltpu.VMEM((1, blk), jnp.int32),
            pltpu.VMEM((1, blk), jnp.int32),
            pltpu.VMEM((8, BS), jnp.int32),
            pltpu.SMEM((8, BS), jnp.int32),
            pltpu.VMEM((blk, rows, share), jnp.float32),
            pltpu.VMEM((slices, 4 * pblk, rows, share), jnp.float32),
            pltpu.VMEM((2, slices, half, rows, share), jnp.float32),
            pltpu.VMEM((2, slices, half, rows, share), jnp.float32),
            pltpu.VMEM((slices, half, rows, share), jnp.float32),
            pltpu.VMEM((slices, half, rows, share), jnp.float32),
            sems((2, 7)), sems((2, 7)),
            sems((slices + 1,)), sems((slices + 1,)), sems((slices + 1,)), sems((slices + 1,)),
            sems((slices + 1,)), sems((slices + 1,)), sems((5,)), sems((5,)), sems((3,)), sems((3,)),
            sems((8,)),
            sems((2, slices)), sems((2, slices)), sems((2, slices)), sems((2, slices)),
            sems((2, slices)), sems((2, slices)),
        ],
        compiler_params=pltpu.CompilerParams(
            collective_id=0, has_side_effects=True, vmem_limit_bytes=48 * 2**20),
        name="gather_factor",
    )(route, slot, pattern, diag, panel.reshape(blk, BS, share), contribution.reshape(blk, BS, share))


def split(value):
    high = value.astype(jnp.bfloat16)
    return high, (value - high.astype(jnp.float32)).astype(jnp.bfloat16)


def store_kernel(parts, f_ref, out_ref, l_ref, f_hbm, out_hbm, l_hbm, sem):
    copies = [pltpu.make_async_copy(l_ref, l_hbm, sem.at[0])]
    for source, target in ((f_ref, f_hbm), (out_ref, out_hbm)):
        n = source.shape[0] // parts
        for k in range(parts):
            part = pl.ds(k * n, n)
            copies.append(pltpu.make_async_copy(source.at[part], target.at[part], sem.at[len(copies)]))
    for copy in copies:
        copy.start()
    for copy in copies:
        copy.wait()


def store(values):
    parts = 1
    return pl.pallas_call(
        functools.partial(store_kernel, parts),
        out_shape=[jax.ShapeDtypeStruct(value.shape, value.dtype) for value in values],
        in_specs=[ANY] * 3,
        out_specs=[ANY] * 3,
        scratch_shapes=[pltpu.SemaphoreType.DMA((2 * parts + 1,))],
        compiler_params=pltpu.CompilerParams(vmem_limit_bytes=2**20),
        name="store",
    )(*values)


def on_small(diag_block, panel, pattern, contribution, route, slot):
    rows, share = panel.shape[1:]
    blk = rows // BS
    factor, assembled, lower = store(factor_and_route(
        route.reshape(1, blk), slot.reshape(1, blk), pattern.reshape(1, blk),
        diag_block[0], panel[0], contribution[0]))
    return (lower[None], factor.reshape(1, rows, share), assembled.reshape(1, rows // 2, share))


def from_root(value, axis, root):
    mine = lax.axis_index(axis) == root
    return lax.psum(jnp.where(mine, value, jnp.zeros_like(value)), axis)


def partner(value, axis, apart):
    mask = 2**apart
    pairs = [(source, source ^ mask) for source in range(lax.axis_size(axis))]
    return lax.ppermute(value, axis, pairs)


def on_large(diag_block, panel, pattern, contribution, route, slot):
    highest = lax.Precision.HIGHEST
    contract = (((1,), (1,)), ((), ()))
    whole = lax.all_gather(diag_block, ("row", "col"), axis=1, tiled=True)[0]
    width = whole.shape[0]
    lower = jnp.linalg.cholesky(whole)
    inverse = jax.scipy.linalg.solve_triangular(
        lower, jnp.eye(width, dtype=jnp.float32), lower=True
    )
    ncol = lax.axis_size("col")
    nrow = lax.axis_size("row")
    col_index = lax.axis_index("col")
    tile_mask = jnp.repeat(jnp.repeat(pattern[0], BS, axis=0), BS, axis=1).astype(jnp.float32)
    masked = panel[0] * tile_mask
    rows_dev = masked.shape[0]
    full_rows = lax.all_gather(masked, "col", axis=1, tiled=True)
    factor_rows = lax.dot_general(full_rows, inverse, contract, precision=highest)
    share = width // ncol
    own_cols = lax.dynamic_slice_in_dim(factor_rows, col_index * share, share, 1)
    cw_dev = contribution.shape[2]
    head_piece = lax.dynamic_slice_in_dim(factor_rows, col_index * cw_dev, cw_dev, 0)
    head_rows = from_root(head_piece, "row", 0)
    update = contribution[0] - lax.dot_general(factor_rows, head_rows, contract, precision=highest)
    blk = rows_dev // BS
    cap = max(2, blk // nrow)
    pblk = blk // 2
    blocks = update.reshape(blk, BS * cw_dev)
    target = route[0, :, 0]
    place = slot[0]
    order_ids = jnp.arange(blk, dtype=jnp.int32)
    earlier = (target[None, :] == target[:, None]) & (order_ids[None, :] < order_ids[:, None])
    rank = jnp.sum(earlier.astype(jnp.int32), axis=1)
    half = target // nrow
    target_row = target % nrow
    position = target_row * (2 * cap) + half * cap + rank
    slots_all = jnp.arange(nrow * 2 * cap, dtype=jnp.int32)
    onehot = (position[None, :] == slots_all[:, None]).astype(jnp.float32)
    packed = jnp.dot(onehot, blocks, precision=highest).reshape(nrow, 2, cap, BS * cw_dev)
    labels = jnp.dot(onehot, (place + 1).astype(jnp.float32), precision=highest).reshape(
        nrow, 2, cap
    )
    mine = lax.axis_index("cube") % 2
    got, got_labels = (
        lax.all_to_all(packed, "row", split_axis=0, concat_axis=0, tiled=True),
        lax.all_to_all(labels, "row", split_axis=0, concat_axis=0, tiled=True),
    )
    keep = lax.dynamic_index_in_dim(got, mine, 1, keepdims=False)
    keep_labels = lax.dynamic_index_in_dim(got_labels, mine, 1, keepdims=False)
    other = lax.dynamic_index_in_dim(got, 1 - mine, 1, keepdims=False)
    other_labels = lax.dynamic_index_in_dim(got_labels, 1 - mine, 1, keepdims=False)
    back, back_labels = partner((other, other_labels), "cube", 0)
    incoming = jnp.concatenate([keep, back], axis=0).reshape(-1, BS * cw_dev)
    tags = jnp.concatenate([keep_labels, back_labels], axis=0).reshape(-1)
    wanted = jnp.arange(1, pblk + 1, dtype=jnp.float32)
    select = (tags[None, :] == wanted[:, None]).astype(jnp.float32)
    assembled = jnp.dot(select, incoming, precision=highest).reshape(pblk * BS, cw_dev)
    rows_here = diag_block.shape[1]
    diag_rows = lax.dynamic_slice_in_dim(
        lower, lax.axis_index(("row", "col")) * rows_here, rows_here, 0
    )
    return (diag_rows[None], own_cols[None], assembled[None])


def solution(mesh):
    small = mesh.shape["row"] == 2 and mesh.shape["col"] == 4
    return jax.shard_map(
        on_small if small else on_large,
        mesh=mesh,
        in_specs=(
            P("cube", ("row", "col"), None),
            P("cube", "row", "col"),
            P("cube", "row", "col"),
            P("cube", "row", "col"),
            P("cube", "row", None),
            P("cube", "row"),
        ),
        out_specs=(
            P("cube", ("row", "col"), None),
            P("cube", "row", "col"),
            P("cube", "row", "col"),
        ),
        check_vma=False,
    )
```

```python
import functools

import jax
import jax.numpy as jnp
from jax import lax
from jax.experimental import pallas as pl
from jax.experimental.pallas import tpu as pltpu
from jax.sharding import PartitionSpec as P

BS = 128
HIGHEST = lax.Precision.HIGHEST
NT = (((1,), (1,)), ((), ()))
TN = (((0,), (0,)), ((), ()))
ANY = pl.BlockSpec(memory_space=pl.ANY)
VMEM = pl.BlockSpec(memory_space=pltpu.VMEM)
MESH = pl.DeviceIdType.MESH


def remote(src, dst, send, recv, device):
    return pltpu.make_async_remote_copy(
        src_ref=src, dst_ref=dst, send_sem=send, recv_sem=recv,
        device_id=device, device_id_type=MESH,
    )


def column(s, j):
    return jnp.take_along_axis(s, jnp.full(s.shape, j, jnp.int32), axis=1)


def factor_block(s_ref, x_ref, middle):
    n, w = BS, 8
    s = s_ref[...]
    for k in range(n // w):
        if k == n // w // 2:
            middle()
        o = w * k
        row = lax.broadcasted_iota(jnp.int32, (w, n), 0)
        lane = lax.broadcasted_iota(jnp.int32, (w, n), 1)
        full, rest = s[:w], s[w:]
        ct = [column(full, o + q) for q in range(w)]
        top = jnp.where((lane >= o) & (lane < o + w), (lane - o == row).astype(jnp.float32), full)
        more = o + w < n
        if more:
            cr = [column(rest, o + q) for q in range(w)]
            lanes = lax.broadcasted_iota(jnp.int32, rest.shape, 1)
            rest = jnp.where((lanes >= o) & (lanes < o + w), 0.0, rest)
        for t in range(0, w, 2):
            c0, c1 = ct[t], ct[t + 1]
            a, b, d = c0[t:t + 1], c1[t:t + 1], c1[t + 1:t + 2]
            inv = 1.0 / (a * d - b * b)
            below = row > t + 1
            m0 = jnp.where(below, (c0 * d - c1 * b) * inv, jnp.where(row == t + 1, b / a, 0.0))
            m1 = jnp.where(below, (c1 * a - c0 * b) * inv, 0.0)
            pairs = [(ct[q][t:t + 1], ct[q][t + 1:t + 2]) for q in range(w)]
            u0, u1 = top[t:t + 1], top[t + 1:t + 2]
            for q in range(t + 2, w):
                ct[q] = ct[q] - (m0 * pairs[q][0] + m1 * pairs[q][1])
            full = full - (m0 * full[t:t + 1] + m1 * full[t + 1:t + 2])
            top = top - (m0 * u0 + m1 * u1)
            if more:
                ai, bi, di = a * inv, b * inv, d * inv
                r0 = cr[t] * di - cr[t + 1] * bi
                r1 = cr[t + 1] * ai - cr[t] * bi
                for q in range(t + 2, w):
                    cr[q] = cr[q] - (r0 * pairs[q][0] + r1 * pairs[q][1])
                rest = rest - (r0 * u0 + r1 * u1)
        s_ref[o:o + w, :] = full
        x_ref[o:o + w, :] = jnp.where(lane <= row + o, top, 0.0)
        s = rest


def cholesky_inverse(a_ref, inv_ref, s_ref, x_ref, r_ref, middle, ready, between):
    width = a_ref.shape[0]
    sub = lax.broadcasted_iota(jnp.int32, (BS, BS), 0)
    lane = lax.broadcasted_iota(jnp.int32, (BS, BS), 1)
    inv_ref[...] = jnp.zeros_like(inv_ref)
    for p in range(width // BS):
        o, e = p * BS, (p + 1) * BS
        if p == 0:
            s_ref[...] = a_ref[o:e, o:e]
        else:
            left = a_ref[:o, o:e]
            s_ref[...] = a_ref[o:e, o:e] - lax.dot_general(left, left, TN, precision=HIGHEST)
            r_ref[:, :o] = -lax.dot_general(left, inv_ref[:o, :o], TN, precision=HIGHEST)
            if e < width:
                r_ref[:, e:] = a_ref[o:e, e:] - lax.dot_general(left, a_ref[:o, e:], TN, precision=HIGHEST)
        factor_block(s_ref, x_ref, middle if p == 0 else (lambda: None))
        if p == 0:
            ready()
        s = s_ref[...]
        d = jnp.sum(jnp.where(lane == sub, s, 0.0), axis=1, keepdims=True)
        rs = 1.0 / jnp.sqrt(d)
        x = x_ref[...] * rs
        a_ref[o:e, o:e] = jnp.where(lane >= sub, s, 0.0) * rs
        inv_ref[o:e, o:e] = x
        if p == 0:
            r_ref[:, e:] = a_ref[o:e, e:]
        if e < width:
            a_ref[o:e, e:] = jnp.dot(x, r_ref[:, e:], precision=HIGHEST)
        if p > 0:
            inv_ref[o:e, :o] = jnp.dot(x, r_ref[:, :o], precision=HIGHEST)
        between(p)


def to_column(row):
    n = row.shape[1]
    sub = lax.broadcasted_iota(jnp.int32, (n, n), 0)
    lane = lax.broadcasted_iota(jnp.int32, (n, n), 1)
    return jnp.sum(jnp.where(sub == lane, row, 0.0), axis=1, keepdims=True)


def chains(goal, slots, table_ref):
    n = goal.shape[1]
    sub = lax.broadcasted_iota(jnp.int32, (n, n), 0)
    lane = lax.broadcasted_iota(jnp.int32, (n, n), 1)
    goal_column = to_column(goal)
    earlier = (goal_column == goal) & (sub < lane)
    number = (sub + 1).astype(jnp.float32)
    prev = jnp.max(jnp.where(earlier, number, 0.0), axis=0, keepdims=True)
    names = lax.broadcasted_iota(jnp.int32, (n, slots), 1).astype(jnp.float32)
    number = (lax.broadcasted_iota(jnp.int32, (n, slots), 0) + 1).astype(jnp.float32)
    last = jnp.max(jnp.where(goal_column == names, number, 0.0), axis=0, keepdims=True)
    table_ref[...] = jnp.zeros_like(table_ref)
    table_ref[0:1, 0:n] = prev.astype(jnp.int32)
    table_ref[1:2, 0:slots] = last.astype(jnp.int32)


def gather_kernel(rows, route_ref, slot_ref, pattern_ref, diag_ref, panel_ref, contribution_ref,
                  f_ref, out_ref, l_ref,
                  own, g0, g1, g2, contrib, a_ref, inv_ref, s_ref, x_ref, r_ref, hh_ref, h_ref, hc_ref, v_ref,
                  vh_ref, vl_ref, masks, head_masks, pats, head_pats, pattern, route, slot, table, names, acc, upd, t_ref, ra, rb, ra2, rb2,
                  dsend, drecv, xsend, xrecv, fsend, frecv, psend, precv, hsend, hrecv,
                  msend, mrecv, isem, asend, arecv, bsend, brecv, lsend, lrecv):
    z = lax.axis_index("cube")
    m = z % 2
    r, c = lax.axis_index("row"), lax.axis_index("col")
    y = 1 - r
    c1 = c + 1 - 2 * (c % 2)
    c2 = (c + 2) % 4
    c3 = (c1 + 2) % 4
    order = (c, c1, c2, c3)
    pieces = (own, g0, g1, g2)
    ndiag, width = diag_ref.shape
    blocks = panel_ref.shape[0]
    slices = BS // rows
    slots = out_ref.shape[0]
    half = slots // 2
    heads = width // BS
    to_x, to_core, to_row = {"col": c2}, {"col": c1}, {"row": y}
    to_cube = {"cube": z + 1 - 2 * m}

    def spot(rr, cc, k):
        return (pl.ds(pl.multiple_of((rr * 4 + cc) * ndiag, ndiag), ndiag),
                pl.ds(0, BS) if k == 0 else pl.ds(BS, width - BS))

    load_own = pltpu.make_async_copy(panel_ref, own, isem.at[0])
    load_contrib = pltpu.make_async_copy(contribution_ref, contrib, isem.at[1])
    load_diag = [pltpu.make_async_copy(
        diag_ref.at[:, spot(r, c, k)[1]], a_ref.at[spot(r, c, k)], isem.at[2 + k]) for k in range(2)]
    load_table = pltpu.make_async_copy(table, names, isem.at[4])
    load_small = [pltpu.make_async_copy(source, target, isem.at[5 + k]) for k, (source, target) in enumerate(
        ((pattern_ref, pattern), (route_ref, route), (slot_ref, slot)))]
    for copy in load_small + load_diag:
        copy.start()
    pats[...] = jnp.zeros_like(pats)
    barrier = pltpu.get_barrier_semaphore()
    for device in (to_x, to_core, to_row, to_cube):
        pl.semaphore_signal(barrier, inc=1, device_id=device, device_id_type=MESH)
    for copy in load_small:
        copy.wait()
    pats[0, 0:1, 0:blocks] = pattern[...].astype(jnp.float32)
    pl.semaphore_wait(barrier, 4)

    def spread(source, target):
        for j in range(4):
            target[j] = jnp.broadcast_to(to_column(source[j, 0:1, 0:blocks]), target.shape[1:])


    def even(rr, cc, k):
        return spot(rr, cc, k)[0], pl.ds(pl.multiple_of((cc // 2 + 2 * k) * BS, BS), BS)

    def piece_copy(k, n, part, device):
        return remote(a_ref.at[part], a_ref.at[part], dsend.at[k, n], drecv.at[k, n], device)

    def own_copy(k, n, part, device):
        return remote(diag_ref.at[:, part[1]], a_ref.at[part], dsend.at[k, n], drecv.at[k, n], device)

    diag = [(own_copy(k, 0, even(r, c, k), to_x), own_copy(k, 1, spot(r, c, k), to_row),
             piece_copy(k, 2, even(r, c2, k), to_row), own_copy(k, 3, spot(r, c, k), to_core),
             piece_copy(k, 4, even(r, c2, k), to_core), piece_copy(k, 5, spot(y, c, k), to_core),
             piece_copy(k, 6, even(y, c2, k), to_core)) for k in range(2)]

    def sliced(i):
        return (pl.ds(heads, blocks - heads), pl.ds(pl.multiple_of(i * rows, rows), rows))

    top = (pl.ds(0, heads),)

    def across(i, part):
        return remote(panel_ref.at[part], g1.at[part], xsend.at[i], xrecv.at[i], to_x)

    def onward(i, part):
        return remote(g1.at[part], g2.at[part], fsend.at[i], frecv.at[i], to_core)

    def beside(i, part):
        return remote(panel_ref.at[part], g0.at[part], psend.at[i], precv.at[i], to_core)

    pair = pl.ds(2 * (c // 2), 2)
    head = [remote(source.at[pair], hh_ref.at[k], hsend.at[k], hrecv.at[k], to_row)
            for k, source in enumerate((panel_ref, g1))]
    swap = [remote(hh_ref.at[k, 1 - c % 2], h_ref.at[k], hsend.at[2 + k], hrecv.at[2 + k], to_core) for k in range(2)]
    mask_x = remote(pats.at[0], pats.at[2], msend.at[0], mrecv.at[0], to_x)
    mask_core = remote(pats.at[0], pats.at[1], msend.at[1], mrecv.at[1], to_core)
    mask_on = remote(pats.at[2], pats.at[3], msend.at[2], mrecv.at[2], to_core)

    for k in range(2):
        for n in (0, 1, 3):
            diag[k][n].start()
    mask_x.start()

    @pl.when(r == 0)
    def _():
        head[0].start()

    across(slices, top).start()
    for i in range(slices):
        across(i, sliced(i)).start()
    mask_core.start()
    beside(slices, top).start()
    for k in range(2):
        diag[k][0].wait_recv()
        diag[k][2].start()
        diag[k][4].start()
        diag[k][1].wait_recv()
        diag[k][5].start()
        if k == 0:
            diag[k][2].wait_recv()
            diag[k][6].start()
            for n in (3, 4, 5, 6):
                diag[k][n].wait_recv()
    for copy in load_diag:
        copy.wait()
    load_own.start()

    def middle():
        diag[1][2].wait_recv()
        diag[1][6].start()

    def ready():
        for n in (3, 4, 5, 6):
            diag[1][n].wait_recv()
        for copies in diag:
            for copy in copies:
                copy.wait_send()

        def mirror(i, j):
            a_ref[i * BS:(i + 1) * BS, j * BS:(j + 1) * BS] = jnp.transpose(
                a_ref[j * BS:(j + 1) * BS, i * BS:(i + 1) * BS])

        for side in range(2):
            @pl.when(c // 2 == side)
            def _():
                for i in range(1 - side, heads, 2):
                    for j in range(i + 1, heads, 2):
                        mirror(i, j)

    head_mask = remote(pats, head_pats, hsend.at[4], hrecv.at[4], to_row)

    def project(p):
        o, e = p * BS, (p + 1) * BS
        line = inv_ref[o:e, :e]
        part = lax.dot_general(line, hc_ref[:, :e], NT, precision=HIGHEST)
        term = lax.dot_general(line, part, TN, precision=HIGHEST)
        if o:
            v_ref[:o] = v_ref[:o] + term[:o]
        v_ref[o:e] = term[o:]

    def between(p):
        if p == 0:
            across(slices, top).wait_recv()
            onward(slices, top).start()

            @pl.when(r == 0)
            def _():
                head[1].start()

            mask_x.wait_recv()
            mask_on.start()
            for i in range(slices):
                beside(i, sliced(i)).start()
            chains((route[...] * slots + slot[...]).astype(jnp.float32), 4 * slots, table)
            load_table.start()
        if p == 1:
            load_own.wait()
            load_contrib.start()
            beside(slices, top).wait_recv()
            onward(slices, top).wait_recv()
            mask_core.wait_recv()
            mask_on.wait_recv()
            spread(pats, masks)

            @pl.when(r == 0)
            def _():
                head_mask.start()
                for j, k in enumerate(order):
                    hc_ref[:, pl.ds(pl.multiple_of(k * BS, BS), BS)] = pieces[j][c] * masks[j, pl.ds(c, 1), :]

            @pl.when(r == 1)
            def _():
                for k in range(2):
                    head[k].wait_recv()
                    swap[k].start()

        if p == 2:
            @pl.when(r == 1)
            def _():
                for copy in swap:
                    copy.wait_recv()
                head_mask.wait_recv()
                spread(head_pats, head_masks)
                heads_in = (hh_ref[0, c % 2], h_ref[0], hh_ref[1, c % 2], h_ref[1])
                for j, k in enumerate(order):
                    hc_ref[:, pl.ds(pl.multiple_of(k * BS, BS), BS)] = heads_in[j] * head_masks[j, pl.ds(c, 1), :]

            for q in range(3):
                project(q)
        if p == 3:
            project(3)

    cholesky_inverse(a_ref, inv_ref, s_ref, x_ref, r_ref, middle, ready, between)
    for j, k in enumerate(order):
        at = pl.ds(pl.multiple_of(k * BS, BS), BS)
        side = jnp.transpose(inv_ref[pl.ds(pl.multiple_of(c * BS, BS), BS), at])
        for q, value in ((0, side), (BS, v_ref[at, :])):
            high, low = split(value)
            vh_ref[j * BS:(j + 1) * BS, q:q + BS] = high
            vl_ref[j * BS:(j + 1) * BS, q:q + BS] = low

    def lower_rows():
        p = 2 * r + c // 2
        for k in range(heads):
            block = jnp.transpose(a_ref[k * BS:(k + 1) * BS, pl.ds(pl.multiple_of(p * BS, BS), BS)])
            s_ref[...] = jnp.where(k <= p, block, 0.0)
            l_ref[:, k * BS:(k + 1) * BS] = s_ref[pl.ds(pl.multiple_of((c % 2) * ndiag, ndiag), ndiag), :]

    load_table.wait()
    load_contrib.wait()
    def product(i, first):
        part = pl.ds(pl.multiple_of(i * rows, rows), rows)
        lines = []
        for at in range(blocks):
            lines.append(jnp.concatenate(
                [pieces[j][at, part] * masks[j, pl.ds(at, 1), :] for j in (first, first + 1)], axis=1))
        high, low = split(jnp.concatenate(lines, axis=0))
        dot = functools.partial(jnp.dot, preferred_element_type=jnp.float32)
        side = slice(first * BS, (first + 2) * BS)
        return dot(high, vh_ref[side]) + (dot(high, vl_ref[side]) + dot(low, vh_ref[side]))

    def early(i):
        part = pl.ds(pl.multiple_of(i * rows, rows), rows)
        out = product(i, 0)
        for at in range(blocks):
            f_ref[at, part] = out[at * rows:(at + 1) * rows, :BS]
            acc[at] = contrib[at, part] - out[at * rows:(at + 1) * rows, BS:]

    def late(i):
        part = pl.ds(pl.multiple_of(i * rows, rows), rows)
        out = product(i, 2)
        for at in range(blocks):
            f_ref[at, part] = f_ref[at, part] + out[at * rows:(at + 1) * rows, :BS]
            update = acc[at] - out[at * rows:(at + 1) * rows, BS:]
            name = names[0, at]
            upd[at] = update + jnp.where(name > 0, 1.0, 0.0) * upd[jnp.clip(name - 1, 0, blocks - 1)]

    def fill(i, start):
        def body(q, carry):
            for b in range(16):
                k = start + q * 16 + b
                name = names[1, k]
                t_ref[i, k] = upd[jnp.clip(name - 1, 0, blocks - 1)] * jnp.where(name > 0, 1.0, 0.0)
            return carry

        lax.fori_loop(0, half // 16, body, 0)

    def quarter(g, low):
        return pl.ds(g * slots + (0 if low else half), half)

    def hops(i):
        goal = ((1 - m) * 2 + y, m * 2 + y, (1 - m) * 2 + r)
        over_a = [remote(t_ref.at[i, quarter(goal[k], True)], ra.at[k, i],
                         asend.at[k, i], arecv.at[k, i], to_row) for k in range(2)]
        over_b = [remote(t_ref.at[i, quarter(goal[2 * k], False)], rb.at[k, i],
                         bsend.at[k, i], brecv.at[k, i], to_cube) for k in range(2)]
        last = [remote(ra.at[0, i], ra2.at[i], lsend.at[0, i], lrecv.at[0, i], to_cube),
                remote(rb.at[0, i], rb2.at[i], lsend.at[1, i], lrecv.at[1, i], to_row)]
        return over_a, over_b, last

    def turn(i):
        over_a, over_b, last = hops(i)
        over_a[0].wait_recv()
        ra[0, i] = ra[0, i] + t_ref[i, quarter((1 - m) * 2 + r, True)]
        last[0].start()
        over_b[0].wait_recv()
        rb[0, i] = rb[0, i] + t_ref[i, quarter(m * 2 + y, False)]
        last[1].start()

    def finish(i):
        part = pl.ds(pl.multiple_of(i * rows, rows), rows)
        over_a, over_b, last = hops(i)
        over_a[1].wait_recv()
        last[0].wait_recv()
        out_ref[pl.ds(0, half), part] = t_ref[i, quarter(m * 2 + r, True)] + ra[1, i] + ra2[i]
        over_b[1].wait_recv()
        last[1].wait_recv()
        out_ref[pl.ds(half, half), part] = t_ref[i, quarter(m * 2 + r, False)] + rb[1, i] + rb2[i]

    upd[...] = jnp.zeros_like(upd)

    def step(i, carry):
        @pl.when(i == 3)
        def _():
            lower_rows()

        @pl.when(i < slices)
        def _():
            beside(i, sliced(i)).wait_recv()
            early(i)
            across(i, sliced(i)).wait_recv()
            onward(i, sliced(i)).start()

        @pl.when(i == slices - 1)
        def _():
            turn(i - 1)

        @pl.when(i < slices)
        def _():
            onward(i, sliced(i)).wait_recv()
            late(i)
            over_a, over_b, _ = hops(i)
            here, there, above = (m * 2 + y) * slots, ((1 - m) * 2 + y) * slots, ((1 - m) * 2 + r) * slots
            fill(i, there)
            over_a[0].start()
            fill(i, there + half)
            over_b[0].start()
            fill(i, here)
            over_a[1].start()
            fill(i, above + half)
            over_b[1].start()
            for start in (above, here + half, (m * 2 + r) * slots, (m * 2 + r) * slots + half):
                fill(i, start)

        @pl.when((i > 0) & (i <= slices) & (i != slices - 1))
        def _():
            turn(i - 1)

        @pl.when(i > 2)
        def _():
            finish(i - 3)

        @pl.when(i > 3)
        def _():
            drain(i - 4)
        return carry

    def drain(i):
        over_a, over_b, last = hops(i)
        for copy in over_a + over_b + last + [across(i, sliced(i)), onward(i, sliced(i)), beside(i, sliced(i))]:
            copy.wait_send()

    lax.fori_loop(0, slices + 3, step, 0)

    for i in (slices - 1,):
        drain(i)
    for copy in (across(slices, top), onward(slices, top), beside(slices, top), mask_x, mask_core, mask_on):
        copy.wait_send()

    @pl.when(r == 0)
    def _():
        for copy in head:
            copy.wait_send()
        head_mask.wait_send()

    @pl.when(r == 1)
    def _():
        for copy in swap:
            copy.wait_send()


def factor_and_route(route, slot, pattern, diag, panel, contribution):
    rows = 8
    slices = BS // rows
    tall, share = panel.shape
    blk = tall // BS
    pblk = blk // 2
    half = pblk // 2
    ndiag, width = diag.shape
    whole = pltpu.VMEM((blk, BS, share), jnp.float32)
    square = pltpu.VMEM((width, width), jnp.float32)
    block = pltpu.VMEM((BS, BS), jnp.float32)
    sems = pltpu.SemaphoreType.DMA
    return pl.pallas_call(
        functools.partial(gather_kernel, rows),
        out_shape=(
            pltpu.VMEM((blk, BS, share), jnp.float32),
            pltpu.VMEM((pblk, BS, share), jnp.float32),
            pltpu.VMEM((ndiag, width), jnp.float32),
        ),
        in_specs=[ANY] * 6,
        out_specs=(VMEM, VMEM, VMEM),
        scratch_shapes=[
            whole, whole, whole, whole, whole,
            square, square, block, block,
            pltpu.VMEM((BS, width), jnp.float32),
            pltpu.VMEM((2, 2, BS, BS), jnp.float32),
            pltpu.VMEM((2, BS, BS), jnp.float32),
            pltpu.VMEM((BS, width), jnp.float32),
            pltpu.VMEM((width, BS), jnp.float32),
            pltpu.VMEM((width, 2 * BS), jnp.bfloat16),
            pltpu.VMEM((width, 2 * BS), jnp.bfloat16),
            pltpu.VMEM((4, blk, share), jnp.float32),
            pltpu.VMEM((4, blk, share), jnp.float32),
            pltpu.VMEM((4, 8, BS), jnp.float32),
            pltpu.VMEM((4, 8, BS), jnp.float32),
            pltpu.VMEM((1, blk), jnp.int32),
            pltpu.VMEM((1, blk), jnp.int32),
            pltpu.VMEM((1, blk), jnp.int32),
            pltpu.VMEM((8, BS), jnp.int32),
            pltpu.SMEM((8, BS), jnp.int32),
            pltpu.VMEM((blk, rows, share), jnp.float32),
            pltpu.VMEM((blk, rows, share), jnp.float32),
            pltpu.VMEM((slices, 4 * pblk, rows, share), jnp.float32),
            pltpu.VMEM((2, slices, half, rows, share), jnp.float32),
            pltpu.VMEM((2, slices, half, rows, share), jnp.float32),
            pltpu.VMEM((slices, half, rows, share), jnp.float32),
            pltpu.VMEM((slices, half, rows, share), jnp.float32),
            sems((2, 7)), sems((2, 7)),
            sems((slices + 1,)), sems((slices + 1,)), sems((slices + 1,)), sems((slices + 1,)),
            sems((slices + 1,)), sems((slices + 1,)), sems((5,)), sems((5,)), sems((3,)), sems((3,)),
            sems((8,)),
            sems((2, slices)), sems((2, slices)), sems((2, slices)), sems((2, slices)),
            sems((2, slices)), sems((2, slices)),
        ],
        compiler_params=pltpu.CompilerParams(
            collective_id=0, has_side_effects=True, vmem_limit_bytes=48 * 2**20),
        name="gather_factor",
    )(route, slot, pattern, diag, panel.reshape(blk, BS, share), contribution.reshape(blk, BS, share))


def split(value):
    high = value.astype(jnp.bfloat16)
    return high, (value - high.astype(jnp.float32)).astype(jnp.bfloat16)


def store_kernel(parts, f_ref, out_ref, l_ref, f_hbm, out_hbm, l_hbm, sem):
    copies = [pltpu.make_async_copy(l_ref, l_hbm, sem.at[0])]
    for source, target in ((f_ref, f_hbm), (out_ref, out_hbm)):
        n = source.shape[0] // parts
        for k in range(parts):
            part = pl.ds(k * n, n)
            copies.append(pltpu.make_async_copy(source.at[part], target.at[part], sem.at[len(copies)]))
    for copy in copies:
        copy.start()
    for copy in copies:
        copy.wait()


def store(values):
    parts = 1
    return pl.pallas_call(
        functools.partial(store_kernel, parts),
        out_shape=[jax.ShapeDtypeStruct(value.shape, value.dtype) for value in values],
        in_specs=[ANY] * 3,
        out_specs=[ANY] * 3,
        scratch_shapes=[pltpu.SemaphoreType.DMA((2 * parts + 1,))],
        compiler_params=pltpu.CompilerParams(vmem_limit_bytes=2**20),
        name="store",
    )(*values)


def on_small(diag_block, panel, pattern, contribution, route, slot):
    rows, share = panel.shape[1:]
    blk = rows // BS
    factor, assembled, lower = store(factor_and_route(
        route.reshape(1, blk), slot.reshape(1, blk), pattern.reshape(1, blk),
        diag_block[0], panel[0], contribution[0]))
    return (lower[None], factor.reshape(1, rows, share), assembled.reshape(1, rows // 2, share))


def from_root(value, axis, root):
    mine = lax.axis_index(axis) == root
    return lax.psum(jnp.where(mine, value, jnp.zeros_like(value)), axis)


def partner(value, axis, apart):
    mask = 2**apart
    pairs = [(source, source ^ mask) for source in range(lax.axis_size(axis))]
    return lax.ppermute(value, axis, pairs)


def on_large(diag_block, panel, pattern, contribution, route, slot):
    highest = lax.Precision.HIGHEST
    contract = (((1,), (1,)), ((), ()))
    whole = lax.all_gather(diag_block, ("row", "col"), axis=1, tiled=True)[0]
    width = whole.shape[0]
    lower = jnp.linalg.cholesky(whole)
    inverse = jax.scipy.linalg.solve_triangular(
        lower, jnp.eye(width, dtype=jnp.float32), lower=True
    )
    ncol = lax.axis_size("col")
    nrow = lax.axis_size("row")
    col_index = lax.axis_index("col")
    tile_mask = jnp.repeat(jnp.repeat(pattern[0], BS, axis=0), BS, axis=1).astype(jnp.float32)
    masked = panel[0] * tile_mask
    rows_dev = masked.shape[0]
    full_rows = lax.all_gather(masked, "col", axis=1, tiled=True)
    factor_rows = lax.dot_general(full_rows, inverse, contract, precision=highest)
    share = width // ncol
    own_cols = lax.dynamic_slice_in_dim(factor_rows, col_index * share, share, 1)
    cw_dev = contribution.shape[2]
    head_piece = lax.dynamic_slice_in_dim(factor_rows, col_index * cw_dev, cw_dev, 0)
    head_rows = from_root(head_piece, "row", 0)
    update = contribution[0] - lax.dot_general(factor_rows, head_rows, contract, precision=highest)
    blk = rows_dev // BS
    cap = max(2, blk // nrow)
    pblk = blk // 2
    blocks = update.reshape(blk, BS * cw_dev)
    target = route[0, :, 0]
    place = slot[0]
    order_ids = jnp.arange(blk, dtype=jnp.int32)
    earlier = (target[None, :] == target[:, None]) & (order_ids[None, :] < order_ids[:, None])
    rank = jnp.sum(earlier.astype(jnp.int32), axis=1)
    half = target // nrow
    target_row = target % nrow
    position = target_row * (2 * cap) + half * cap + rank
    slots_all = jnp.arange(nrow * 2 * cap, dtype=jnp.int32)
    onehot = (position[None, :] == slots_all[:, None]).astype(jnp.float32)
    packed = jnp.dot(onehot, blocks, precision=highest).reshape(nrow, 2, cap, BS * cw_dev)
    labels = jnp.dot(onehot, (place + 1).astype(jnp.float32), precision=highest).reshape(
        nrow, 2, cap
    )
    mine = lax.axis_index("cube") % 2
    got, got_labels = (
        lax.all_to_all(packed, "row", split_axis=0, concat_axis=0, tiled=True),
        lax.all_to_all(labels, "row", split_axis=0, concat_axis=0, tiled=True),
    )
    keep = lax.dynamic_index_in_dim(got, mine, 1, keepdims=False)
    keep_labels = lax.dynamic_index_in_dim(got_labels, mine, 1, keepdims=False)
    other = lax.dynamic_index_in_dim(got, 1 - mine, 1, keepdims=False)
    other_labels = lax.dynamic_index_in_dim(got_labels, 1 - mine, 1, keepdims=False)
    back, back_labels = partner((other, other_labels), "cube", 0)
    incoming = jnp.concatenate([keep, back], axis=0).reshape(-1, BS * cw_dev)
    tags = jnp.concatenate([keep_labels, back_labels], axis=0).reshape(-1)
    wanted = jnp.arange(1, pblk + 1, dtype=jnp.float32)
    select = (tags[None, :] == wanted[:, None]).astype(jnp.float32)
    assembled = jnp.dot(select, incoming, precision=highest).reshape(pblk * BS, cw_dev)
    rows_here = diag_block.shape[1]
    diag_rows = lax.dynamic_slice_in_dim(
        lower, lax.axis_index(("row", "col")) * rows_here, rows_here, 0
    )
    return (diag_rows[None], own_cols[None], assembled[None])


def solution(mesh):
    small = mesh.shape["row"] == 2 and mesh.shape["col"] == 4
    return jax.shard_map(
        on_small if small else on_large,
        mesh=mesh,
        in_specs=(
            P("cube", ("row", "col"), None),
            P("cube", "row", "col"),
            P("cube", "row", "col"),
            P("cube", "row", "col"),
            P("cube", "row", None),
            P("cube", "row"),
        ),
        out_specs=(
            P("cube", ("row", "col"), None),
            P("cube", "row", "col"),
            P("cube", "row", "col"),
        ),
        check_vma=False,
    )
```

```python
import functools

import jax
import jax.numpy as jnp
from jax import lax
from jax.experimental import pallas as pl
from jax.experimental.pallas import tpu as pltpu
from jax.sharding import PartitionSpec as P

BS = 128
HIGHEST = lax.Precision.HIGHEST
NT = (((1,), (1,)), ((), ()))
TN = (((0,), (0,)), ((), ()))
ANY = pl.BlockSpec(memory_space=pl.ANY)
VMEM = pl.BlockSpec(memory_space=pltpu.VMEM)
MESH = pl.DeviceIdType.MESH


def remote(src, dst, send, recv, device):
    return pltpu.make_async_remote_copy(
        src_ref=src, dst_ref=dst, send_sem=send, recv_sem=recv,
        device_id=device, device_id_type=MESH,
    )


def column(s, j):
    return jnp.take_along_axis(s, jnp.full(s.shape, j, jnp.int32), axis=1)


def factor_block(s_ref, x_ref, middle):
    n, w = BS, 8
    s = s_ref[...]
    for k in range(n // w):
        if k == n // w // 2:
            middle()
        o = w * k
        row = lax.broadcasted_iota(jnp.int32, (w, n), 0)
        lane = lax.broadcasted_iota(jnp.int32, (w, n), 1)
        full, rest = s[:w], s[w:]
        ct = [column(full, o + q) for q in range(w)]
        top = jnp.where((lane >= o) & (lane < o + w), (lane - o == row).astype(jnp.float32), full)
        more = o + w < n
        if more:
            cr = [column(rest, o + q) for q in range(w)]
            lanes = lax.broadcasted_iota(jnp.int32, rest.shape, 1)
            rest = jnp.where((lanes >= o) & (lanes < o + w), 0.0, rest)
        for t in range(0, w, 2):
            c0, c1 = ct[t], ct[t + 1]
            a, b, d = c0[t:t + 1], c1[t:t + 1], c1[t + 1:t + 2]
            inv = 1.0 / (a * d - b * b)
            below = row > t + 1
            m0 = jnp.where(below, (c0 * d - c1 * b) * inv, jnp.where(row == t + 1, b / a, 0.0))
            m1 = jnp.where(below, (c1 * a - c0 * b) * inv, 0.0)
            pairs = [(ct[q][t:t + 1], ct[q][t + 1:t + 2]) for q in range(w)]
            u0, u1 = top[t:t + 1], top[t + 1:t + 2]
            for q in range(t + 2, w):
                ct[q] = ct[q] - (m0 * pairs[q][0] + m1 * pairs[q][1])
            full = full - (m0 * full[t:t + 1] + m1 * full[t + 1:t + 2])
            top = top - (m0 * u0 + m1 * u1)
            if more:
                ai, bi, di = a * inv, b * inv, d * inv
                r0 = cr[t] * di - cr[t + 1] * bi
                r1 = cr[t + 1] * ai - cr[t] * bi
                for q in range(t + 2, w):
                    cr[q] = cr[q] - (r0 * pairs[q][0] + r1 * pairs[q][1])
                rest = rest - (r0 * u0 + r1 * u1)
        s_ref[o:o + w, :] = full
        x_ref[o:o + w, :] = jnp.where(lane <= row + o, top, 0.0)
        s = rest


def cholesky_inverse(a_ref, inv_ref, s_ref, x_ref, r_ref, middle, ready, between):
    width = a_ref.shape[0]
    sub = lax.broadcasted_iota(jnp.int32, (BS, BS), 0)
    lane = lax.broadcasted_iota(jnp.int32, (BS, BS), 1)
    inv_ref[...] = jnp.zeros_like(inv_ref)
    for p in range(width // BS):
        o, e = p * BS, (p + 1) * BS
        if p == 0:
            s_ref[...] = a_ref[o:e, o:e]
        else:
            left = a_ref[:o, o:e]
            s_ref[...] = a_ref[o:e, o:e] - lax.dot_general(left, left, TN, precision=HIGHEST)
            r_ref[:, :o] = -lax.dot_general(left, inv_ref[:o, :o], TN, precision=HIGHEST)
            if e < width:
                r_ref[:, e:] = a_ref[o:e, e:] - lax.dot_general(left, a_ref[:o, e:], TN, precision=HIGHEST)
        factor_block(s_ref, x_ref, middle if p == 0 else (lambda: None))
        if p == 0:
            ready()
        s = s_ref[...]
        d = jnp.sum(jnp.where(lane == sub, s, 0.0), axis=1, keepdims=True)
        rs = 1.0 / jnp.sqrt(d)
        x = x_ref[...] * rs
        a_ref[o:e, o:e] = jnp.where(lane >= sub, s, 0.0) * rs
        inv_ref[o:e, o:e] = x
        if p == 0:
            r_ref[:, e:] = a_ref[o:e, e:]
        if e < width:
            a_ref[o:e, e:] = jnp.dot(x, r_ref[:, e:], precision=HIGHEST)
        if p > 0:
            inv_ref[o:e, :o] = jnp.dot(x, r_ref[:, :o], precision=HIGHEST)
        between(p)


def to_column(row):
    n = row.shape[1]
    sub = lax.broadcasted_iota(jnp.int32, (n, n), 0)
    lane = lax.broadcasted_iota(jnp.int32, (n, n), 1)
    return jnp.sum(jnp.where(sub == lane, row, 0.0), axis=1, keepdims=True)


def chains(goal, slots, table_ref):
    n = goal.shape[1]
    sub = lax.broadcasted_iota(jnp.int32, (n, n), 0)
    lane = lax.broadcasted_iota(jnp.int32, (n, n), 1)
    goal_column = to_column(goal)
    earlier = (goal_column == goal) & (sub < lane)
    number = (sub + 1).astype(jnp.float32)
    prev = jnp.max(jnp.where(earlier, number, 0.0), axis=0, keepdims=True)
    names = lax.broadcasted_iota(jnp.int32, (n, slots), 1).astype(jnp.float32)
    number = (lax.broadcasted_iota(jnp.int32, (n, slots), 0) + 1).astype(jnp.float32)
    last = jnp.max(jnp.where(goal_column == names, number, 0.0), axis=0, keepdims=True)
    table_ref[...] = jnp.zeros_like(table_ref)
    table_ref[0:1, 0:n] = prev.astype(jnp.int32)
    table_ref[1:2, 0:slots] = last.astype(jnp.int32)


def gather_kernel(rows, route_ref, slot_ref, pattern_ref, diag_ref, panel_ref, contribution_ref,
                  f_ref, out_ref, l_ref,
                  own, g0, g1, g2, contrib, a_ref, inv_ref, s_ref, x_ref, r_ref, hh_ref, h_ref, hc_ref, v_ref,
                  vh_ref, vl_ref, masks, head_masks, pats, head_pats, pattern, route, slot, table, names, acc, upd, t_ref, ra, rb, ra2, rb2,
                  dsend, drecv, xsend, xrecv, fsend, frecv, psend, precv, hsend, hrecv,
                  msend, mrecv, isem, asend, arecv, bsend, brecv, lsend, lrecv):
    z = lax.axis_index("cube")
    m = z % 2
    r, c = lax.axis_index("row"), lax.axis_index("col")
    y = 1 - r
    c1 = c + 1 - 2 * (c % 2)
    c2 = (c + 2) % 4
    c3 = (c1 + 2) % 4
    order = (c, c1, c2, c3)
    pieces = (own, g0, g1, g2)
    ndiag, width = diag_ref.shape
    blocks = panel_ref.shape[0]
    slices = BS // rows
    slots = out_ref.shape[0]
    half = slots // 2
    heads = width // BS
    to_x, to_core, to_row = {"col": c2}, {"col": c1}, {"row": y}
    to_cube = {"cube": z + 1 - 2 * m}

    def spot(rr, cc, k):
        return (pl.ds(pl.multiple_of((rr * 4 + cc) * ndiag, ndiag), ndiag),
                pl.ds(0, BS) if k == 0 else pl.ds(BS, width - BS))

    load_own = pltpu.make_async_copy(panel_ref, own, isem.at[0])
    load_contrib = pltpu.make_async_copy(contribution_ref, contrib, isem.at[1])
    load_diag = [pltpu.make_async_copy(
        diag_ref.at[:, spot(r, c, k)[1]], a_ref.at[spot(r, c, k)], isem.at[2 + k]) for k in range(2)]
    load_table = pltpu.make_async_copy(table, names, isem.at[4])
    load_small = [pltpu.make_async_copy(source, target, isem.at[5 + k]) for k, (source, target) in enumerate(
        ((pattern_ref, pattern), (route_ref, route), (slot_ref, slot)))]
    barrier = pltpu.get_barrier_semaphore()
    for device in (to_x, to_core, to_row, to_cube):
        pl.semaphore_signal(barrier, inc=1, device_id=device, device_id_type=MESH)
    for copy in load_small + load_diag:
        copy.start()
    pats[0] = jnp.zeros(pats.shape[1:], jnp.float32)
    pl.semaphore_wait(barrier, 4)

    def spread(source, target):
        for j in range(4):
            target[j] = jnp.broadcast_to(to_column(source[j, 0:1, 0:blocks]), target.shape[1:])


    def even(rr, cc, k):
        return spot(rr, cc, k)[0], pl.ds(pl.multiple_of((cc // 2 + 2 * k) * BS, BS), BS)

    def piece_copy(k, n, part, device):
        return remote(a_ref.at[part], a_ref.at[part], dsend.at[k, n], drecv.at[k, n], device)

    def own_copy(k, n, part, device):
        return remote(diag_ref.at[:, part[1]], a_ref.at[part], dsend.at[k, n], drecv.at[k, n], device)

    diag = [(own_copy(k, 0, even(r, c, k), to_x), own_copy(k, 1, spot(r, c, k), to_row),
             piece_copy(k, 2, even(r, c2, k), to_row), own_copy(k, 3, spot(r, c, k), to_core),
             piece_copy(k, 4, even(r, c2, k), to_core), piece_copy(k, 5, spot(y, c, k), to_core),
             piece_copy(k, 6, even(y, c2, k), to_core)) for k in range(2)]

    def sliced(i):
        return (pl.ds(heads, blocks - heads), pl.ds(pl.multiple_of(i * rows, rows), rows))

    top = (pl.ds(0, heads),)

    def across(i, part):
        return remote(panel_ref.at[part], g1.at[part], xsend.at[i], xrecv.at[i], to_x)

    def onward(i, part):
        return remote(g1.at[part], g2.at[part], fsend.at[i], frecv.at[i], to_core)

    def beside(i, part):
        return remote(panel_ref.at[part], g0.at[part], psend.at[i], precv.at[i], to_core)

    pair = pl.ds(2 * (c // 2), 2)
    head = [remote(source.at[pair], hh_ref.at[k], hsend.at[k], hrecv.at[k], to_row)
            for k, source in enumerate((panel_ref, g1))]
    swap = [remote(hh_ref.at[k, 1 - c % 2], h_ref.at[k], hsend.at[2 + k], hrecv.at[2 + k], to_core) for k in range(2)]
    mask_x = remote(pats.at[0], pats.at[2], msend.at[0], mrecv.at[0], to_x)
    mask_core = remote(pats.at[0], pats.at[1], msend.at[1], mrecv.at[1], to_core)
    mask_on = remote(pats.at[2], pats.at[3], msend.at[2], mrecv.at[2], to_core)

    for k in range(2):
        for n in (0, 1, 3):
            diag[k][n].start()

    @pl.when(r == 0)
    def _():
        head[0].start()

    across(slices, top).start()
    for copy in load_small:
        copy.wait()
    pats[0, 0:1, 0:blocks] = pattern[...].astype(jnp.float32)
    mask_x.start()
    for i in range(slices):
        across(i, sliced(i)).start()
    mask_core.start()
    beside(slices, top).start()
    for k in range(2):
        diag[k][0].wait_recv()
        diag[k][2].start()
        diag[k][4].start()
        diag[k][1].wait_recv()
        diag[k][5].start()
        if k == 0:
            diag[k][2].wait_recv()
            diag[k][6].start()
            for n in (3, 4, 5, 6):
                diag[k][n].wait_recv()
    for copy in load_diag:
        copy.wait()
    load_own.start()

    def middle():
        diag[1][2].wait_recv()
        diag[1][6].start()

    def ready():
        for n in (3, 4, 5, 6):
            diag[1][n].wait_recv()
        for copies in diag:
            for copy in copies:
                copy.wait_send()

        def mirror(i, j):
            a_ref[i * BS:(i + 1) * BS, j * BS:(j + 1) * BS] = jnp.transpose(
                a_ref[j * BS:(j + 1) * BS, i * BS:(i + 1) * BS])

        for side in range(2):
            @pl.when(c // 2 == side)
            def _():
                for i in range(1 - side, heads, 2):
                    for j in range(i + 1, heads, 2):
                        mirror(i, j)

    head_mask = remote(pats, head_pats, hsend.at[4], hrecv.at[4], to_row)

    def project(p):
        o, e = p * BS, (p + 1) * BS
        line = inv_ref[o:e, :e]
        part = lax.dot_general(line, hc_ref[:, :e], NT, precision=HIGHEST)
        term = lax.dot_general(line, part, TN, precision=HIGHEST)
        if o:
            v_ref[:o] = v_ref[:o] + term[:o]
        v_ref[o:e] = term[o:]

    def between(p):
        if p == 0:
            across(slices, top).wait_recv()
            onward(slices, top).start()

            @pl.when(r == 0)
            def _():
                head[1].start()

            mask_x.wait_recv()
            mask_on.start()
            for i in range(slices):
                beside(i, sliced(i)).start()
            chains((route[...] * slots + slot[...]).astype(jnp.float32), 4 * slots, table)
            load_table.start()
        if p == 1:
            load_own.wait()
            load_contrib.start()
            beside(slices, top).wait_recv()
            onward(slices, top).wait_recv()
            mask_core.wait_recv()
            mask_on.wait_recv()
            spread(pats, masks)

            @pl.when(r == 0)
            def _():
                head_mask.start()
                for j, k in enumerate(order):
                    hc_ref[:, pl.ds(pl.multiple_of(k * BS, BS), BS)] = pieces[j][c] * masks[j, pl.ds(c, 1), :]

            @pl.when(r == 1)
            def _():
                for k in range(2):
                    head[k].wait_recv()
                    swap[k].start()

        if p == 2:
            @pl.when(r == 1)
            def _():
                for copy in swap:
                    copy.wait_recv()
                head_mask.wait_recv()
                spread(head_pats, head_masks)
                heads_in = (hh_ref[0, c % 2], h_ref[0], hh_ref[1, c % 2], h_ref[1])
                for j, k in enumerate(order):
                    hc_ref[:, pl.ds(pl.multiple_of(k * BS, BS), BS)] = heads_in[j] * head_masks[j, pl.ds(c, 1), :]

            for q in range(3):
                project(q)
        if p == 3:
            project(3)

    cholesky_inverse(a_ref, inv_ref, s_ref, x_ref, r_ref, middle, ready, between)
    for j, k in enumerate(order):
        at = pl.ds(pl.multiple_of(k * BS, BS), BS)
        side = jnp.transpose(inv_ref[pl.ds(pl.multiple_of(c * BS, BS), BS), at])
        for q, value in ((0, side), (BS, v_ref[at, :])):
            high, low = split(value)
            vh_ref[j * BS:(j + 1) * BS, q:q + BS] = high
            vl_ref[j * BS:(j + 1) * BS, q:q + BS] = low

    def lower_rows():
        p = 2 * r + c // 2
        for k in range(heads):
            block = jnp.transpose(a_ref[k * BS:(k + 1) * BS, pl.ds(pl.multiple_of(p * BS, BS), BS)])
            s_ref[...] = jnp.where(k <= p, block, 0.0)
            l_ref[:, k * BS:(k + 1) * BS] = s_ref[pl.ds(pl.multiple_of((c % 2) * ndiag, ndiag), ndiag), :]

    load_table.wait()
    load_contrib.wait()
    def product(i, first):
        part = pl.ds(pl.multiple_of(i * rows, rows), rows)
        lines = []
        for at in range(blocks):
            lines.append(jnp.concatenate(
                [pieces[j][at, part] * masks[j, pl.ds(at, 1), :] for j in (first, first + 1)], axis=1))
        high, low = split(jnp.concatenate(lines, axis=0))
        dot = functools.partial(jnp.dot, preferred_element_type=jnp.float32)
        side = slice(first * BS, (first + 2) * BS)
        return dot(high, vh_ref[side]) + (dot(high, vl_ref[side]) + dot(low, vh_ref[side]))

    def early(i):
        part = pl.ds(pl.multiple_of(i * rows, rows), rows)
        out = product(i, 0)
        for at in range(blocks):
            f_ref[at, part] = out[at * rows:(at + 1) * rows, :BS]
            acc[at] = contrib[at, part] - out[at * rows:(at + 1) * rows, BS:]

    def late(i):
        part = pl.ds(pl.multiple_of(i * rows, rows), rows)
        out = product(i, 2)
        for at in range(blocks):
            f_ref[at, part] = f_ref[at, part] + out[at * rows:(at + 1) * rows, :BS]
            update = acc[at] - out[at * rows:(at + 1) * rows, BS:]
            name = names[0, at]
            upd[at] = update + jnp.where(name > 0, 1.0, 0.0) * upd[jnp.clip(name - 1, 0, blocks - 1)]

    def fill(i, start):
        def body(q, carry):
            for b in range(16):
                k = start + q * 16 + b
                name = names[1, k]
                t_ref[i, k] = upd[jnp.clip(name - 1, 0, blocks - 1)] * jnp.where(name > 0, 1.0, 0.0)
            return carry

        lax.fori_loop(0, half // 16, body, 0)

    def quarter(g, low):
        return pl.ds(g * slots + (0 if low else half), half)

    def hops(i):
        goal = ((1 - m) * 2 + y, m * 2 + y, (1 - m) * 2 + r)
        over_a = [remote(t_ref.at[i, quarter(goal[k], True)], ra.at[k, i],
                         asend.at[k, i], arecv.at[k, i], to_row) for k in range(2)]
        over_b = [remote(t_ref.at[i, quarter(goal[2 * k], False)], rb.at[k, i],
                         bsend.at[k, i], brecv.at[k, i], to_cube) for k in range(2)]
        last = [remote(ra.at[0, i], ra2.at[i], lsend.at[0, i], lrecv.at[0, i], to_cube),
                remote(rb.at[0, i], rb2.at[i], lsend.at[1, i], lrecv.at[1, i], to_row)]
        return over_a, over_b, last

    def turn(i):
        over_a, over_b, last = hops(i)
        over_a[0].wait_recv()
        ra[0, i] = ra[0, i] + t_ref[i, quarter((1 - m) * 2 + r, True)]
        last[0].start()
        over_b[0].wait_recv()
        rb[0, i] = rb[0, i] + t_ref[i, quarter(m * 2 + y, False)]
        last[1].start()

    def finish(i):
        part = pl.ds(pl.multiple_of(i * rows, rows), rows)
        over_a, over_b, last = hops(i)
        over_a[1].wait_recv()
        last[0].wait_recv()
        out_ref[pl.ds(0, half), part] = t_ref[i, quarter(m * 2 + r, True)] + ra[1, i] + ra2[i]
        over_b[1].wait_recv()
        last[1].wait_recv()
        out_ref[pl.ds(half, half), part] = t_ref[i, quarter(m * 2 + r, False)] + rb[1, i] + rb2[i]

    upd[...] = jnp.zeros_like(upd)

    def step(i, carry):
        @pl.when(i == 3)
        def _():
            lower_rows()

        @pl.when(i < slices)
        def _():
            beside(i, sliced(i)).wait_recv()
            early(i)
            across(i, sliced(i)).wait_recv()
            onward(i, sliced(i)).start()

        @pl.when(i == slices - 1)
        def _():
            turn(i - 1)

        @pl.when(i < slices)
        def _():
            onward(i, sliced(i)).wait_recv()
            late(i)
            over_a, over_b, _ = hops(i)
            here, there, above = (m * 2 + y) * slots, ((1 - m) * 2 + y) * slots, ((1 - m) * 2 + r) * slots
            fill(i, there)
            over_a[0].start()
            fill(i, there + half)
            over_b[0].start()
            fill(i, here)
            over_a[1].start()
            fill(i, above + half)
            over_b[1].start()
            for start in (above, here + half, (m * 2 + r) * slots, (m * 2 + r) * slots + half):
                fill(i, start)

        @pl.when((i > 0) & (i <= slices) & (i != slices - 1))
        def _():
            turn(i - 1)

        @pl.when(i > 2)
        def _():
            finish(i - 3)

        @pl.when(i > 3)
        def _():
            drain(i - 4)
        return carry

    def drain(i):
        over_a, over_b, last = hops(i)
        for copy in over_a + over_b + last + [across(i, sliced(i)), onward(i, sliced(i)), beside(i, sliced(i))]:
            copy.wait_send()

    lax.fori_loop(0, slices + 3, step, 0)

    for i in (slices - 1,):
        drain(i)
    for copy in (across(slices, top), onward(slices, top), beside(slices, top), mask_x, mask_core, mask_on):
        copy.wait_send()

    @pl.when(r == 0)
    def _():
        for copy in head:
            copy.wait_send()
        head_mask.wait_send()

    @pl.when(r == 1)
    def _():
        for copy in swap:
            copy.wait_send()


def factor_and_route(route, slot, pattern, diag, panel, contribution):
    rows = 8
    slices = BS // rows
    tall, share = panel.shape
    blk = tall // BS
    pblk = blk // 2
    half = pblk // 2
    ndiag, width = diag.shape
    whole = pltpu.VMEM((blk, BS, share), jnp.float32)
    square = pltpu.VMEM((width, width), jnp.float32)
    block = pltpu.VMEM((BS, BS), jnp.float32)
    sems = pltpu.SemaphoreType.DMA
    return pl.pallas_call(
        functools.partial(gather_kernel, rows),
        out_shape=(
            pltpu.VMEM((blk, BS, share), jnp.float32),
            pltpu.VMEM((pblk, BS, share), jnp.float32),
            pltpu.VMEM((ndiag, width), jnp.float32),
        ),
        in_specs=[ANY] * 6,
        out_specs=(VMEM, VMEM, VMEM),
        scratch_shapes=[
            whole, whole, whole, whole, whole,
            square, square, block, block,
            pltpu.VMEM((BS, width), jnp.float32),
            pltpu.VMEM((2, 2, BS, BS), jnp.float32),
            pltpu.VMEM((2, BS, BS), jnp.float32),
            pltpu.VMEM((BS, width), jnp.float32),
            pltpu.VMEM((width, BS), jnp.float32),
            pltpu.VMEM((width, 2 * BS), jnp.bfloat16),
            pltpu.VMEM((width, 2 * BS), jnp.bfloat16),
            pltpu.VMEM((4, blk, share), jnp.float32),
            pltpu.VMEM((4, blk, share), jnp.float32),
            pltpu.VMEM((4, 8, BS), jnp.float32),
            pltpu.VMEM((4, 8, BS), jnp.float32),
            pltpu.VMEM((1, blk), jnp.int32),
            pltpu.VMEM((1, blk), jnp.int32),
            pltpu.VMEM((1, blk), jnp.int32),
            pltpu.VMEM((8, BS), jnp.int32),
            pltpu.SMEM((8, BS), jnp.int32),
            pltpu.VMEM((blk, rows, share), jnp.float32),
            pltpu.VMEM((blk, rows, share), jnp.float32),
            pltpu.VMEM((slices, 4 * pblk, rows, share), jnp.float32),
            pltpu.VMEM((2, slices, half, rows, share), jnp.float32),
            pltpu.VMEM((2, slices, half, rows, share), jnp.float32),
            pltpu.VMEM((slices, half, rows, share), jnp.float32),
            pltpu.VMEM((slices, half, rows, share), jnp.float32),
            sems((2, 7)), sems((2, 7)),
            sems((slices + 1,)), sems((slices + 1,)), sems((slices + 1,)), sems((slices + 1,)),
            sems((slices + 1,)), sems((slices + 1,)), sems((5,)), sems((5,)), sems((3,)), sems((3,)),
            sems((8,)),
            sems((2, slices)), sems((2, slices)), sems((2, slices)), sems((2, slices)),
            sems((2, slices)), sems((2, slices)),
        ],
        compiler_params=pltpu.CompilerParams(
            collective_id=0, has_side_effects=True, vmem_limit_bytes=48 * 2**20),
        name="gather_factor",
    )(route, slot, pattern, diag, panel.reshape(blk, BS, share), contribution.reshape(blk, BS, share))


def split(value):
    high = value.astype(jnp.bfloat16)
    return high, (value - high.astype(jnp.float32)).astype(jnp.bfloat16)


def store_kernel(parts, f_ref, out_ref, l_ref, f_hbm, out_hbm, l_hbm, sem):
    copies = [pltpu.make_async_copy(l_ref, l_hbm, sem.at[0])]
    for source, target in ((f_ref, f_hbm), (out_ref, out_hbm)):
        n = source.shape[0] // parts
        for k in range(parts):
            part = pl.ds(k * n, n)
            copies.append(pltpu.make_async_copy(source.at[part], target.at[part], sem.at[len(copies)]))
    for copy in copies:
        copy.start()
    for copy in copies:
        copy.wait()


def store(values):
    parts = 1
    return pl.pallas_call(
        functools.partial(store_kernel, parts),
        out_shape=[jax.ShapeDtypeStruct(value.shape, value.dtype) for value in values],
        in_specs=[ANY] * 3,
        out_specs=[ANY] * 3,
        scratch_shapes=[pltpu.SemaphoreType.DMA((2 * parts + 1,))],
        compiler_params=pltpu.CompilerParams(vmem_limit_bytes=2**20),
        name="store",
    )(*values)


def on_small(diag_block, panel, pattern, contribution, route, slot):
    rows, share = panel.shape[1:]
    blk = rows // BS
    factor, assembled, lower = store(factor_and_route(
        route.reshape(1, blk), slot.reshape(1, blk), pattern.reshape(1, blk),
        diag_block[0], panel[0], contribution[0]))
    return (lower[None], factor.reshape(1, rows, share), assembled.reshape(1, rows // 2, share))


def from_root(value, axis, root):
    mine = lax.axis_index(axis) == root
    return lax.psum(jnp.where(mine, value, jnp.zeros_like(value)), axis)


def partner(value, axis, apart):
    mask = 2**apart
    pairs = [(source, source ^ mask) for source in range(lax.axis_size(axis))]
    return lax.ppermute(value, axis, pairs)


def on_large(diag_block, panel, pattern, contribution, route, slot):
    highest = lax.Precision.HIGHEST
    contract = (((1,), (1,)), ((), ()))
    whole = lax.all_gather(diag_block, ("row", "col"), axis=1, tiled=True)[0]
    width = whole.shape[0]
    lower = jnp.linalg.cholesky(whole)
    inverse = jax.scipy.linalg.solve_triangular(
        lower, jnp.eye(width, dtype=jnp.float32), lower=True
    )
    ncol = lax.axis_size("col")
    nrow = lax.axis_size("row")
    col_index = lax.axis_index("col")
    tile_mask = jnp.repeat(jnp.repeat(pattern[0], BS, axis=0), BS, axis=1).astype(jnp.float32)
    masked = panel[0] * tile_mask
    rows_dev = masked.shape[0]
    full_rows = lax.all_gather(masked, "col", axis=1, tiled=True)
    factor_rows = lax.dot_general(full_rows, inverse, contract, precision=highest)
    share = width // ncol
    own_cols = lax.dynamic_slice_in_dim(factor_rows, col_index * share, share, 1)
    cw_dev = contribution.shape[2]
    head_piece = lax.dynamic_slice_in_dim(factor_rows, col_index * cw_dev, cw_dev, 0)
    head_rows = from_root(head_piece, "row", 0)
    update = contribution[0] - lax.dot_general(factor_rows, head_rows, contract, precision=highest)
    blk = rows_dev // BS
    cap = max(2, blk // nrow)
    pblk = blk // 2
    blocks = update.reshape(blk, BS * cw_dev)
    target = route[0, :, 0]
    place = slot[0]
    order_ids = jnp.arange(blk, dtype=jnp.int32)
    earlier = (target[None, :] == target[:, None]) & (order_ids[None, :] < order_ids[:, None])
    rank = jnp.sum(earlier.astype(jnp.int32), axis=1)
    half = target // nrow
    target_row = target % nrow
    position = target_row * (2 * cap) + half * cap + rank
    slots_all = jnp.arange(nrow * 2 * cap, dtype=jnp.int32)
    onehot = (position[None, :] == slots_all[:, None]).astype(jnp.float32)
    packed = jnp.dot(onehot, blocks, precision=highest).reshape(nrow, 2, cap, BS * cw_dev)
    labels = jnp.dot(onehot, (place + 1).astype(jnp.float32), precision=highest).reshape(
        nrow, 2, cap
    )
    mine = lax.axis_index("cube") % 2
    got, got_labels = (
        lax.all_to_all(packed, "row", split_axis=0, concat_axis=0, tiled=True),
        lax.all_to_all(labels, "row", split_axis=0, concat_axis=0, tiled=True),
    )
    keep = lax.dynamic_index_in_dim(got, mine, 1, keepdims=False)
    keep_labels = lax.dynamic_index_in_dim(got_labels, mine, 1, keepdims=False)
    other = lax.dynamic_index_in_dim(got, 1 - mine, 1, keepdims=False)
    other_labels = lax.dynamic_index_in_dim(got_labels, 1 - mine, 1, keepdims=False)
    back, back_labels = partner((other, other_labels), "cube", 0)
    incoming = jnp.concatenate([keep, back], axis=0).reshape(-1, BS * cw_dev)
    tags = jnp.concatenate([keep_labels, back_labels], axis=0).reshape(-1)
    wanted = jnp.arange(1, pblk + 1, dtype=jnp.float32)
    select = (tags[None, :] == wanted[:, None]).astype(jnp.float32)
    assembled = jnp.dot(select, incoming, precision=highest).reshape(pblk * BS, cw_dev)
    rows_here = diag_block.shape[1]
    diag_rows = lax.dynamic_slice_in_dim(
        lower, lax.axis_index(("row", "col")) * rows_here, rows_here, 0
    )
    return (diag_rows[None], own_cols[None], assembled[None])


def solution(mesh):
    small = mesh.shape["row"] == 2 and mesh.shape["col"] == 4
    return jax.shard_map(
        on_small if small else on_large,
        mesh=mesh,
        in_specs=(
            P("cube", ("row", "col"), None),
            P("cube", "row", "col"),
            P("cube", "row", "col"),
            P("cube", "row", "col"),
            P("cube", "row", None),
            P("cube", "row"),
        ),
        out_specs=(
            P("cube", ("row", "col"), None),
            P("cube", "row", "col"),
            P("cube", "row", "col"),
        ),
        check_vma=False,
    )
```

```python
import functools

import jax
import jax.numpy as jnp
from jax import lax
from jax.experimental import pallas as pl
from jax.experimental.pallas import tpu as pltpu
from jax.sharding import PartitionSpec as P

BS = 128
HIGHEST = lax.Precision.HIGHEST
NT = (((1,), (1,)), ((), ()))
TN = (((0,), (0,)), ((), ()))
ANY = pl.BlockSpec(memory_space=pl.ANY)
VMEM = pl.BlockSpec(memory_space=pltpu.VMEM)
MESH = pl.DeviceIdType.MESH


def remote(src, dst, send, recv, device):
    return pltpu.make_async_remote_copy(
        src_ref=src, dst_ref=dst, send_sem=send, recv_sem=recv,
        device_id=device, device_id_type=MESH,
    )


def column(s, j):
    return jnp.take_along_axis(s, jnp.full(s.shape, j, jnp.int32), axis=1)


def factor_block(s_ref, x_ref, middle):
    n, w = BS, 8
    s = s_ref[...]
    for k in range(n // w):
        if k == n // w // 2:
            middle()
        o = w * k
        row = lax.broadcasted_iota(jnp.int32, (w, n), 0)
        lane = lax.broadcasted_iota(jnp.int32, (w, n), 1)
        full, rest = s[:w], s[w:]
        ct = [column(full, o + q) for q in range(w)]
        top = jnp.where((lane >= o) & (lane < o + w), (lane - o == row).astype(jnp.float32), full)
        more = o + w < n
        if more:
            cr = [column(rest, o + q) for q in range(w)]
            lanes = lax.broadcasted_iota(jnp.int32, rest.shape, 1)
            rest = jnp.where((lanes >= o) & (lanes < o + w), 0.0, rest)
        for t in range(0, w, 2):
            c0, c1 = ct[t], ct[t + 1]
            a, b, d = c0[t:t + 1], c1[t:t + 1], c1[t + 1:t + 2]
            inv = 1.0 / (a * d - b * b)
            below = row > t + 1
            m0 = jnp.where(below, (c0 * d - c1 * b) * inv, jnp.where(row == t + 1, b / a, 0.0))
            m1 = jnp.where(below, (c1 * a - c0 * b) * inv, 0.0)
            pairs = [(ct[q][t:t + 1], ct[q][t + 1:t + 2]) for q in range(w)]
            u0, u1 = top[t:t + 1], top[t + 1:t + 2]
            for q in range(t + 2, w):
                ct[q] = ct[q] - (m0 * pairs[q][0] + m1 * pairs[q][1])
            full = full - (m0 * full[t:t + 1] + m1 * full[t + 1:t + 2])
            top = top - (m0 * u0 + m1 * u1)
            if more:
                ai, bi, di = a * inv, b * inv, d * inv
                r0 = cr[t] * di - cr[t + 1] * bi
                r1 = cr[t + 1] * ai - cr[t] * bi
                for q in range(t + 2, w):
                    cr[q] = cr[q] - (r0 * pairs[q][0] + r1 * pairs[q][1])
                rest = rest - (r0 * u0 + r1 * u1)
        s_ref[o:o + w, :] = full
        x_ref[o:o + w, :] = jnp.where(lane <= row + o, top, 0.0)
        s = rest


def cholesky_inverse(a_ref, inv_ref, s_ref, x_ref, r_ref, middle, ready, between):
    width = a_ref.shape[0]
    sub = lax.broadcasted_iota(jnp.int32, (BS, BS), 0)
    lane = lax.broadcasted_iota(jnp.int32, (BS, BS), 1)
    inv_ref[...] = jnp.zeros_like(inv_ref)
    for p in range(width // BS):
        o, e = p * BS, (p + 1) * BS
        if p == 0:
            s_ref[...] = a_ref[o:e, o:e]
        else:
            left = a_ref[:o, o:e]
            s_ref[...] = a_ref[o:e, o:e] - lax.dot_general(left, left, TN, precision=HIGHEST)
            r_ref[:, :o] = -lax.dot_general(left, inv_ref[:o, :o], TN, precision=HIGHEST)
            if e < width:
                r_ref[:, e:] = a_ref[o:e, e:] - lax.dot_general(left, a_ref[:o, e:], TN, precision=HIGHEST)
        factor_block(s_ref, x_ref, middle if p == 0 else (lambda: None))
        if p == 0:
            ready()
        s = s_ref[...]
        d = jnp.sum(jnp.where(lane == sub, s, 0.0), axis=1, keepdims=True)
        rs = 1.0 / jnp.sqrt(d)
        x = x_ref[...] * rs
        a_ref[o:e, o:e] = jnp.where(lane >= sub, s, 0.0) * rs
        inv_ref[o:e, o:e] = x
        if p == 0:
            r_ref[:, e:] = a_ref[o:e, e:]
        if e < width:
            a_ref[o:e, e:] = jnp.dot(x, r_ref[:, e:], precision=HIGHEST)
        if p > 0:
            inv_ref[o:e, :o] = jnp.dot(x, r_ref[:, :o], precision=HIGHEST)
        between(p)


def to_column(row):
    n = row.shape[1]
    sub = lax.broadcasted_iota(jnp.int32, (n, n), 0)
    lane = lax.broadcasted_iota(jnp.int32, (n, n), 1)
    return jnp.sum(jnp.where(sub == lane, row, 0.0), axis=1, keepdims=True)


def chains(goal, slots, table_ref):
    n = goal.shape[1]
    sub = lax.broadcasted_iota(jnp.int32, (n, n), 0)
    lane = lax.broadcasted_iota(jnp.int32, (n, n), 1)
    goal_column = to_column(goal)
    earlier = (goal_column == goal) & (sub < lane)
    number = (sub + 1).astype(jnp.float32)
    prev = jnp.max(jnp.where(earlier, number, 0.0), axis=0, keepdims=True)
    names = lax.broadcasted_iota(jnp.int32, (n, slots), 1).astype(jnp.float32)
    number = (lax.broadcasted_iota(jnp.int32, (n, slots), 0) + 1).astype(jnp.float32)
    last = jnp.max(jnp.where(goal_column == names, number, 0.0), axis=0, keepdims=True)
    table_ref[...] = jnp.zeros_like(table_ref)
    table_ref[0:1, 0:n] = prev.astype(jnp.int32)
    table_ref[1:2, 0:slots] = last.astype(jnp.int32)


def gather_kernel(rows, route_ref, slot_ref, pattern_ref, diag_ref, panel_ref, contribution_ref,
                  f_ref, out_ref, l_ref,
                  own, g0, g1, g2, contrib, a_ref, inv_ref, s_ref, x_ref, r_ref, hh_ref, h_ref, hc_ref, v_ref,
                  vh_ref, vl_ref, masks, head_masks, pats, head_pats, pattern, route, slot, table, names, acc, upd, t_ref, ra, rb, ra2, rb2,
                  dsend, drecv, xsend, xrecv, fsend, frecv, psend, precv, hsend, hrecv,
                  msend, mrecv, isem, asend, arecv, bsend, brecv, lsend, lrecv):
    z = lax.axis_index("cube")
    m = z % 2
    r, c = lax.axis_index("row"), lax.axis_index("col")
    y = 1 - r
    c1 = c + 1 - 2 * (c % 2)
    c2 = (c + 2) % 4
    c3 = (c1 + 2) % 4
    order = (c, c1, c2, c3)
    pieces = (own, g0, g1, g2)
    ndiag, width = diag_ref.shape
    blocks = panel_ref.shape[0]
    slices = BS // rows
    slots = out_ref.shape[0]
    half = slots // 2
    heads = width // BS
    to_x, to_core, to_row = {"col": c2}, {"col": c1}, {"row": y}
    to_cube = {"cube": z + 1 - 2 * m}

    def spot(rr, cc, k):
        return (pl.ds(pl.multiple_of((rr * 4 + cc) * ndiag, ndiag), ndiag),
                pl.ds(0, BS) if k == 0 else pl.ds(BS, width - BS))

    load_own = pltpu.make_async_copy(panel_ref, own, isem.at[0])
    load_contrib = pltpu.make_async_copy(contribution_ref, contrib, isem.at[1])
    load_diag = [pltpu.make_async_copy(
        diag_ref.at[:, spot(r, c, k)[1]], a_ref.at[spot(r, c, k)], isem.at[2 + k]) for k in range(2)]
    load_table = pltpu.make_async_copy(table, names, isem.at[4])
    load_small = [pltpu.make_async_copy(source, target, isem.at[5 + k]) for k, (source, target) in enumerate(
        ((pattern_ref, pattern), (route_ref, route), (slot_ref, slot)))]
    barrier = pltpu.get_barrier_semaphore()
    for device in (to_x, to_core, to_row, to_cube):
        pl.semaphore_signal(barrier, inc=1, device_id=device, device_id_type=MESH)
    for copy in load_small + load_diag:
        copy.start()
    pats[0] = jnp.zeros(pats.shape[1:], jnp.float32)
    pl.semaphore_wait(barrier, 4)

    def spread(source, target):
        for j in range(4):
            target[j] = jnp.broadcast_to(to_column(source[j, 0:1, 0:blocks]), target.shape[1:])


    def even(rr, cc, k):
        return spot(rr, cc, k)[0], pl.ds(pl.multiple_of((cc // 2 + 2 * k) * BS, BS), BS)

    def piece_copy(k, n, part, device):
        return remote(a_ref.at[part], a_ref.at[part], dsend.at[k, n], drecv.at[k, n], device)

    def own_copy(k, n, part, device):
        return remote(diag_ref.at[:, part[1]], a_ref.at[part], dsend.at[k, n], drecv.at[k, n], device)

    diag = [(own_copy(k, 0, even(r, c, k), to_x), own_copy(k, 1, spot(r, c, k), to_row),
             piece_copy(k, 2, even(r, c2, k), to_row), own_copy(k, 3, spot(r, c, k), to_core),
             piece_copy(k, 4, even(r, c2, k), to_core), piece_copy(k, 5, spot(y, c, k), to_core),
             piece_copy(k, 6, even(y, c2, k), to_core)) for k in range(2)]

    def sliced(i):
        return (pl.ds(heads, blocks - heads), pl.ds(pl.multiple_of(i * rows, rows), rows))

    top = (pl.ds(0, heads),)

    def across(i, part):
        return remote(panel_ref.at[part], g1.at[part], xsend.at[i], xrecv.at[i], to_x)

    def onward(i, part):
        return remote(g1.at[part], g2.at[part], fsend.at[i], frecv.at[i], to_core)

    def beside(i, part):
        return remote(panel_ref.at[part], g0.at[part], psend.at[i], precv.at[i], to_core)

    pair = pl.ds(2 * (c // 2), 2)
    head = [remote(source.at[pair], hh_ref.at[k], hsend.at[k], hrecv.at[k], to_row)
            for k, source in enumerate((panel_ref, g1))]
    swap = [remote(hh_ref.at[k, 1 - c % 2], h_ref.at[k], hsend.at[2 + k], hrecv.at[2 + k], to_core) for k in range(2)]
    mask_x = remote(pats.at[0], pats.at[2], msend.at[0], mrecv.at[0], to_x)
    mask_core = remote(pats.at[0], pats.at[1], msend.at[1], mrecv.at[1], to_core)
    mask_on = remote(pats.at[2], pats.at[3], msend.at[2], mrecv.at[2], to_core)

    for k in range(2):
        for n in (0, 1, 3):
            diag[k][n].start()

    @pl.when(r == 0)
    def _():
        head[0].start()

    across(slices, top).start()
    for copy in load_small:
        copy.wait()
    pats[0, 0:1, 0:blocks] = pattern[...].astype(jnp.float32)
    mask_x.start()
    for i in range(slices):
        across(i, sliced(i)).start()
    mask_core.start()
    beside(slices, top).start()
    for k in range(2):
        diag[k][0].wait_recv()
        diag[k][2].start()
        diag[k][4].start()
        diag[k][1].wait_recv()
        diag[k][5].start()
        if k == 0:
            diag[k][2].wait_recv()
            diag[k][6].start()
            for n in (3, 4, 5, 6):
                diag[k][n].wait_recv()
    for copy in load_diag:
        copy.wait()
    load_own.start()

    def middle():
        diag[1][2].wait_recv()
        diag[1][6].start()

    def ready():
        for n in (3, 4, 5, 6):
            diag[1][n].wait_recv()
        for copies in diag:
            for copy in copies:
                copy.wait_send()

        def mirror(i, j):
            a_ref[i * BS:(i + 1) * BS, j * BS:(j + 1) * BS] = jnp.transpose(
                a_ref[j * BS:(j + 1) * BS, i * BS:(i + 1) * BS])

        for side in range(2):
            @pl.when(c // 2 == side)
            def _():
                for i in range(1 - side, heads, 2):
                    for j in range(i + 1, heads, 2):
                        mirror(i, j)

    head_mask = remote(pats, head_pats, hsend.at[4], hrecv.at[4], to_row)

    def project(p):
        o, e = p * BS, (p + 1) * BS
        line = inv_ref[o:e, :e]
        part = lax.dot_general(line, hc_ref[:, :e], NT, precision=HIGHEST)
        term = lax.dot_general(line, part, TN, precision=HIGHEST)
        if o:
            v_ref[:o] = v_ref[:o] + term[:o]
        v_ref[o:e] = term[o:]

    def between(p):
        if p == 0:
            across(slices, top).wait_recv()
            onward(slices, top).start()

            @pl.when(r == 0)
            def _():
                head[1].start()

            mask_x.wait_recv()
            mask_on.start()
            for i in range(slices):
                beside(i, sliced(i)).start()
            chains((route[...] * slots + slot[...]).astype(jnp.float32), 4 * slots, table)
            load_table.start()
        if p == 1:
            load_own.wait()
            load_contrib.start()
            beside(slices, top).wait_recv()
            onward(slices, top).wait_recv()
            mask_core.wait_recv()
            mask_on.wait_recv()
            spread(pats, masks)

            @pl.when(r == 0)
            def _():
                head_mask.start()
                for j, k in enumerate(order):
                    hc_ref[:, pl.ds(pl.multiple_of(k * BS, BS), BS)] = pieces[j][c] * masks[j, pl.ds(c, 1), :]

            @pl.when(r == 1)
            def _():
                for k in range(2):
                    head[k].wait_recv()
                    swap[k].start()

        if p == 2:
            @pl.when(r == 1)
            def _():
                for copy in swap:
                    copy.wait_recv()
                head_mask.wait_recv()
                spread(head_pats, head_masks)
                heads_in = (hh_ref[0, c % 2], h_ref[0], hh_ref[1, c % 2], h_ref[1])
                for j, k in enumerate(order):
                    hc_ref[:, pl.ds(pl.multiple_of(k * BS, BS), BS)] = heads_in[j] * head_masks[j, pl.ds(c, 1), :]

            for q in range(3):
                project(q)
        if p == 3:
            project(3)

    cholesky_inverse(a_ref, inv_ref, s_ref, x_ref, r_ref, middle, ready, between)
    for j, k in enumerate(order):
        at = pl.ds(pl.multiple_of(k * BS, BS), BS)
        side = jnp.transpose(inv_ref[pl.ds(pl.multiple_of(c * BS, BS), BS), at])
        for q, value in ((0, side), (BS, v_ref[at, :])):
            high, low = split(value)
            vh_ref[j * BS:(j + 1) * BS, q:q + BS] = high
            vl_ref[j * BS:(j + 1) * BS, q:q + BS] = low

    def lower_rows():
        p = 2 * r + c // 2
        for k in range(heads):
            block = jnp.transpose(a_ref[k * BS:(k + 1) * BS, pl.ds(pl.multiple_of(p * BS, BS), BS)])
            s_ref[...] = jnp.where(k <= p, block, 0.0)
            l_ref[:, k * BS:(k + 1) * BS] = s_ref[pl.ds(pl.multiple_of((c % 2) * ndiag, ndiag), ndiag), :]

    load_table.wait()
    load_contrib.wait()
    def product(i, first):
        part = pl.ds(pl.multiple_of(i * rows, rows), rows)
        lines = []
        for at in range(blocks):
            lines.append(jnp.concatenate(
                [pieces[j][at, part] * masks[j, pl.ds(at, 1), :] for j in (first, first + 1)], axis=1))
        high, low = split(jnp.concatenate(lines, axis=0))
        dot = functools.partial(jnp.dot, preferred_element_type=jnp.float32)
        side = slice(first * BS, (first + 2) * BS)
        return dot(high, vh_ref[side]) + (dot(high, vl_ref[side]) + dot(low, vh_ref[side]))

    def early(i):
        part = pl.ds(pl.multiple_of(i * rows, rows), rows)
        out = product(i, 0)
        for at in range(blocks):
            f_ref[at, part] = out[at * rows:(at + 1) * rows, :BS]
            acc[at] = contrib[at, part] - out[at * rows:(at + 1) * rows, BS:]

    def late(i):
        part = pl.ds(pl.multiple_of(i * rows, rows), rows)
        out = product(i, 2)
        for at in range(blocks):
            f_ref[at, part] = f_ref[at, part] + out[at * rows:(at + 1) * rows, :BS]
            update = acc[at] - out[at * rows:(at + 1) * rows, BS:]
            name = names[0, at]
            upd[at] = update + jnp.where(name > 0, 1.0, 0.0) * upd[jnp.clip(name - 1, 0, blocks - 1)]

    def fill(i, start):
        def body(q, carry):
            for b in range(16):
                k = start + q * 16 + b
                name = names[1, k]
                t_ref[i, k] = upd[jnp.clip(name - 1, 0, blocks - 1)] * jnp.where(name > 0, 1.0, 0.0)
            return carry

        lax.fori_loop(0, half // 16, body, 0)

    def quarter(g, low):
        return pl.ds(g * slots + (0 if low else half), half)

    def hops(i):
        goal = ((1 - m) * 2 + y, m * 2 + y, (1 - m) * 2 + r)
        over_a = [remote(t_ref.at[i, quarter(goal[k], True)], ra.at[k, i],
                         asend.at[k, i], arecv.at[k, i], to_row) for k in range(2)]
        over_b = [remote(t_ref.at[i, quarter(goal[2 * k], False)], rb.at[k, i],
                         bsend.at[k, i], brecv.at[k, i], to_cube) for k in range(2)]
        last = [remote(ra.at[0, i], ra2.at[i], lsend.at[0, i], lrecv.at[0, i], to_cube),
                remote(rb.at[0, i], rb2.at[i], lsend.at[1, i], lrecv.at[1, i], to_row)]
        return over_a, over_b, last

    def turn(i):
        over_a, over_b, last = hops(i)
        over_a[0].wait_recv()
        ra[0, i] = ra[0, i] + t_ref[i, quarter((1 - m) * 2 + r, True)]
        last[0].start()
        over_b[0].wait_recv()
        rb[0, i] = rb[0, i] + t_ref[i, quarter(m * 2 + y, False)]
        last[1].start()

    def finish(i):
        part = pl.ds(pl.multiple_of(i * rows, rows), rows)
        over_a, over_b, last = hops(i)
        over_a[1].wait_recv()
        last[0].wait_recv()
        out_ref[pl.ds(0, half), part] = t_ref[i, quarter(m * 2 + r, True)] + ra[1, i] + ra2[i]
        over_b[1].wait_recv()
        last[1].wait_recv()
        out_ref[pl.ds(half, half), part] = t_ref[i, quarter(m * 2 + r, False)] + rb[1, i] + rb2[i]

    upd[...] = jnp.zeros_like(upd)

    def settle():
        for copy in (across(slices, top), onward(slices, top), beside(slices, top), mask_x, mask_core, mask_on):
            copy.wait_send()

        @pl.when(r == 0)
        def _():
            for copy in head:
                copy.wait_send()
            head_mask.wait_send()

        @pl.when(r == 1)
        def _():
            for copy in swap:
                copy.wait_send()

    def step(i, carry):
        @pl.when(i == 3)
        def _():
            lower_rows()
            settle()

        @pl.when(i < slices)
        def _():
            beside(i, sliced(i)).wait_recv()
            early(i)
            across(i, sliced(i)).wait_recv()
            onward(i, sliced(i)).start()

        @pl.when(i == slices - 1)
        def _():
            turn(i - 1)

        @pl.when(i < slices)
        def _():
            onward(i, sliced(i)).wait_recv()
            late(i)
            over_a, over_b, _ = hops(i)
            here, there, above = (m * 2 + y) * slots, ((1 - m) * 2 + y) * slots, ((1 - m) * 2 + r) * slots
            fill(i, there)
            over_a[0].start()
            fill(i, there + half)
            over_b[0].start()
            fill(i, here)
            over_a[1].start()
            fill(i, above + half)
            over_b[1].start()
            for start in (above, here + half, (m * 2 + r) * slots, (m * 2 + r) * slots + half):
                fill(i, start)

        @pl.when((i > 0) & (i <= slices) & (i != slices - 1))
        def _():
            turn(i - 1)

        @pl.when(i > 2)
        def _():
            finish(i - 3)

        @pl.when(i > 2)
        def _():
            drain(i - 3)
        return carry

    def drain(i):
        over_a, over_b, last = hops(i)
        for copy in over_a + over_b + last + [across(i, sliced(i)), onward(i, sliced(i)), beside(i, sliced(i))]:
            copy.wait_send()

    lax.fori_loop(0, slices + 3, step, 0)


def factor_and_route(route, slot, pattern, diag, panel, contribution):
    rows = 8
    slices = BS // rows
    tall, share = panel.shape
    blk = tall // BS
    pblk = blk // 2
    half = pblk // 2
    ndiag, width = diag.shape
    whole = pltpu.VMEM((blk, BS, share), jnp.float32)
    square = pltpu.VMEM((width, width), jnp.float32)
    block = pltpu.VMEM((BS, BS), jnp.float32)
    sems = pltpu.SemaphoreType.DMA
    return pl.pallas_call(
        functools.partial(gather_kernel, rows),
        out_shape=(
            pltpu.VMEM((blk, BS, share), jnp.float32),
            pltpu.VMEM((pblk, BS, share), jnp.float32),
            pltpu.VMEM((ndiag, width), jnp.float32),
        ),
        in_specs=[ANY] * 6,
        out_specs=(VMEM, VMEM, VMEM),
        scratch_shapes=[
            whole, whole, whole, whole, whole,
            square, square, block, block,
            pltpu.VMEM((BS, width), jnp.float32),
            pltpu.VMEM((2, 2, BS, BS), jnp.float32),
            pltpu.VMEM((2, BS, BS), jnp.float32),
            pltpu.VMEM((BS, width), jnp.float32),
            pltpu.VMEM((width, BS), jnp.float32),
            pltpu.VMEM((width, 2 * BS), jnp.bfloat16),
            pltpu.VMEM((width, 2 * BS), jnp.bfloat16),
            pltpu.VMEM((4, blk, share), jnp.float32),
            pltpu.VMEM((4, blk, share), jnp.float32),
            pltpu.VMEM((4, 8, BS), jnp.float32),
            pltpu.VMEM((4, 8, BS), jnp.float32),
            pltpu.VMEM((1, blk), jnp.int32),
            pltpu.VMEM((1, blk), jnp.int32),
            pltpu.VMEM((1, blk), jnp.int32),
            pltpu.VMEM((8, BS), jnp.int32),
            pltpu.SMEM((8, BS), jnp.int32),
            pltpu.VMEM((blk, rows, share), jnp.float32),
            pltpu.VMEM((blk, rows, share), jnp.float32),
            pltpu.VMEM((slices, 4 * pblk, rows, share), jnp.float32),
            pltpu.VMEM((2, slices, half, rows, share), jnp.float32),
            pltpu.VMEM((2, slices, half, rows, share), jnp.float32),
            pltpu.VMEM((slices, half, rows, share), jnp.float32),
            pltpu.VMEM((slices, half, rows, share), jnp.float32),
            sems((2, 7)), sems((2, 7)),
            sems((slices + 1,)), sems((slices + 1,)), sems((slices + 1,)), sems((slices + 1,)),
            sems((slices + 1,)), sems((slices + 1,)), sems((5,)), sems((5,)), sems((3,)), sems((3,)),
            sems((8,)),
            sems((2, slices)), sems((2, slices)), sems((2, slices)), sems((2, slices)),
            sems((2, slices)), sems((2, slices)),
        ],
        compiler_params=pltpu.CompilerParams(
            collective_id=0, has_side_effects=True, vmem_limit_bytes=48 * 2**20),
        name="gather_factor",
    )(route, slot, pattern, diag, panel.reshape(blk, BS, share), contribution.reshape(blk, BS, share))


def split(value):
    high = value.astype(jnp.bfloat16)
    return high, (value - high.astype(jnp.float32)).astype(jnp.bfloat16)


def store_kernel(parts, f_ref, out_ref, l_ref, f_hbm, out_hbm, l_hbm, sem):
    copies = [pltpu.make_async_copy(l_ref, l_hbm, sem.at[0])]
    for source, target in ((f_ref, f_hbm), (out_ref, out_hbm)):
        n = source.shape[0] // parts
        for k in range(parts):
            part = pl.ds(k * n, n)
            copies.append(pltpu.make_async_copy(source.at[part], target.at[part], sem.at[len(copies)]))
    for copy in copies:
        copy.start()
    for copy in copies:
        copy.wait()


def store(values):
    parts = 1
    return pl.pallas_call(
        functools.partial(store_kernel, parts),
        out_shape=[jax.ShapeDtypeStruct(value.shape, value.dtype) for value in values],
        in_specs=[ANY] * 3,
        out_specs=[ANY] * 3,
        scratch_shapes=[pltpu.SemaphoreType.DMA((2 * parts + 1,))],
        compiler_params=pltpu.CompilerParams(vmem_limit_bytes=2**20),
        name="store",
    )(*values)


def on_small(diag_block, panel, pattern, contribution, route, slot):
    rows, share = panel.shape[1:]
    blk = rows // BS
    factor, assembled, lower = store(factor_and_route(
        route.reshape(1, blk), slot.reshape(1, blk), pattern.reshape(1, blk),
        diag_block[0], panel[0], contribution[0]))
    return (lower[None], factor.reshape(1, rows, share), assembled.reshape(1, rows // 2, share))


def from_root(value, axis, root):
    mine = lax.axis_index(axis) == root
    return lax.psum(jnp.where(mine, value, jnp.zeros_like(value)), axis)


def partner(value, axis, apart):
    mask = 2**apart
    pairs = [(source, source ^ mask) for source in range(lax.axis_size(axis))]
    return lax.ppermute(value, axis, pairs)


def on_large(diag_block, panel, pattern, contribution, route, slot):
    highest = lax.Precision.HIGHEST
    contract = (((1,), (1,)), ((), ()))
    whole = lax.all_gather(diag_block, ("row", "col"), axis=1, tiled=True)[0]
    width = whole.shape[0]
    lower = jnp.linalg.cholesky(whole)
    inverse = jax.scipy.linalg.solve_triangular(
        lower, jnp.eye(width, dtype=jnp.float32), lower=True
    )
    ncol = lax.axis_size("col")
    nrow = lax.axis_size("row")
    col_index = lax.axis_index("col")
    tile_mask = jnp.repeat(jnp.repeat(pattern[0], BS, axis=0), BS, axis=1).astype(jnp.float32)
    masked = panel[0] * tile_mask
    rows_dev = masked.shape[0]
    full_rows = lax.all_gather(masked, "col", axis=1, tiled=True)
    factor_rows = lax.dot_general(full_rows, inverse, contract, precision=highest)
    share = width // ncol
    own_cols = lax.dynamic_slice_in_dim(factor_rows, col_index * share, share, 1)
    cw_dev = contribution.shape[2]
    head_piece = lax.dynamic_slice_in_dim(factor_rows, col_index * cw_dev, cw_dev, 0)
    head_rows = from_root(head_piece, "row", 0)
    update = contribution[0] - lax.dot_general(factor_rows, head_rows, contract, precision=highest)
    blk = rows_dev // BS
    cap = max(2, blk // nrow)
    pblk = blk // 2
    blocks = update.reshape(blk, BS * cw_dev)
    target = route[0, :, 0]
    place = slot[0]
    order_ids = jnp.arange(blk, dtype=jnp.int32)
    earlier = (target[None, :] == target[:, None]) & (order_ids[None, :] < order_ids[:, None])
    rank = jnp.sum(earlier.astype(jnp.int32), axis=1)
    half = target // nrow
    target_row = target % nrow
    position = target_row * (2 * cap) + half * cap + rank
    slots_all = jnp.arange(nrow * 2 * cap, dtype=jnp.int32)
    onehot = (position[None, :] == slots_all[:, None]).astype(jnp.float32)
    packed = jnp.dot(onehot, blocks, precision=highest).reshape(nrow, 2, cap, BS * cw_dev)
    labels = jnp.dot(onehot, (place + 1).astype(jnp.float32), precision=highest).reshape(
        nrow, 2, cap
    )
    mine = lax.axis_index("cube") % 2
    got, got_labels = (
        lax.all_to_all(packed, "row", split_axis=0, concat_axis=0, tiled=True),
        lax.all_to_all(labels, "row", split_axis=0, concat_axis=0, tiled=True),
    )
    keep = lax.dynamic_index_in_dim(got, mine, 1, keepdims=False)
    keep_labels = lax.dynamic_index_in_dim(got_labels, mine, 1, keepdims=False)
    other = lax.dynamic_index_in_dim(got, 1 - mine, 1, keepdims=False)
    other_labels = lax.dynamic_index_in_dim(got_labels, 1 - mine, 1, keepdims=False)
    back, back_labels = partner((other, other_labels), "cube", 0)
    incoming = jnp.concatenate([keep, back], axis=0).reshape(-1, BS * cw_dev)
    tags = jnp.concatenate([keep_labels, back_labels], axis=0).reshape(-1)
    wanted = jnp.arange(1, pblk + 1, dtype=jnp.float32)
    select = (tags[None, :] == wanted[:, None]).astype(jnp.float32)
    assembled = jnp.dot(select, incoming, precision=highest).reshape(pblk * BS, cw_dev)
    rows_here = diag_block.shape[1]
    diag_rows = lax.dynamic_slice_in_dim(
        lower, lax.axis_index(("row", "col")) * rows_here, rows_here, 0
    )
    return (diag_rows[None], own_cols[None], assembled[None])


def solution(mesh):
    small = mesh.shape["row"] == 2 and mesh.shape["col"] == 4
    return jax.shard_map(
        on_small if small else on_large,
        mesh=mesh,
        in_specs=(
            P("cube", ("row", "col"), None),
            P("cube", "row", "col"),
            P("cube", "row", "col"),
            P("cube", "row", "col"),
            P("cube", "row", None),
            P("cube", "row"),
        ),
        out_specs=(
            P("cube", ("row", "col"), None),
            P("cube", "row", "col"),
            P("cube", "row", "col"),
        ),
        check_vma=False,
    )
```
